256 devices in a mesh: seq: 32 (over x, y, core), head: 8 (over z).
Axes of the slice: x: 4, y: 4, z: 8, core: 2. Of those that a mesh axis runs over, the one named last changes fastest.
Arguments:
- tokens: bfloat16 [32768, 2048], P('seq', 'head'), may hold values from -6 to 6
- seg_ids: int32 [32768], replicated, may hold values from 0 to 31, never falling along the last dimension, each value on 1 to 16384 neighbouring positions
- w_gate: bfloat16 [2048, 4096], P(None, 'head'), may hold values from -0.125 to 0.125
- w_x: bfloat16 [2048, 4096], P(None, 'head'), may hold values from -0.125 to 0.125
- w_bc: bfloat16 [2048, 256], replicated, may hold values from -0.125 to 0.125
- w_dt: bfloat16 [2048, 64], P(None, 'head'), may hold values from -0.125 to 0.125
- conv_x: float32 [4, 4096], P(None, 'head'), may hold values from -3 to 3
- conv_bc: float32 [4, 256], replicated, may hold values from -3 to 3
- conv_x_bias: float32 [4096], P('head'), may hold values from -3 to 3
- conv_bc_bias: float32 [256], replicated, may hold values from -3 to 3
- dt_bias: float32 [64], P('head'), may hold values from -4 to -1
- decay_rate: float32 [64], P('head'), may hold values from 0.0002 to 4
- skip_gain: float32 [64], P('head'), may hold values from 0.5 to 1.5
- norm_gain: float32 [4096], P('head'), may hold values from 0.5 to 1.5
- w_out: bfloat16 [4096, 2048], P('head'), may hold values from -0.125 to 0.125
Outputs:
- mixed: bfloat16 [32768, 2048], P('seq', 'head')
- end_state: float32 [32, 64, 64, 128], P('seq', 'head')
The draws below stay inside these ranges and needn't reach their ends.
Inputs may be any that keep to these rules, and one draw needn't show every extreme that they name: `seg_ids`: prompt numbers never fall along the tokens; each prompt holds 1 to 16384 tokens, one of them exactly 16384.
All inputs are finite; a program needn't handle non-finite values.
Results may differ from the reference program's by a relative error of at most 0.0075.
Values may be sent and summed in bfloat16 or wider, within the bound.
A program may use at most 128 MiB of HBM per device.

```python
import math
import jax
import jax.numpy as jnp
import numpy as np
from jax import lax

D = 2048
HEADS = 64
HEAD_DIM = 64
STATE = 128
CONV = 4
GROUP = 256
REQS = 32
TOK_DEV = 1024
INNER = 4096
TOKENS = 32768
LONG = 16384


def strengthened(values, rng, source, target, parts, factor):
    owner, partner = [(jnp.arange(values.shape[axis_at]) // (values.shape[axis_at] // parts)).reshape([-1 if axis == axis_at else 1 for axis in range(values.ndim)]) for axis_at in (source, target)]
    chosen = jax.random.permutation(rng, parts)[partner]
    strong = (owner == chosen) | (owner == (partner + parts // 2) % parts)
    return jnp.where(strong, factor * values, values)


def steps_of(stream_key, extent, pieces, smallest, high):
    loudness, own = 1.0, jax.random.fold_in(stream_key, 6)
    for dim, parts in pieces:
        steps = jnp.exp(jax.random.uniform(jax.random.fold_in(own, dim), (parts,), jnp.float32, smallest / len(pieces), high / len(pieces)))
        loudness = loudness * jnp.repeat(steps, extent[dim] // parts).reshape([-1 if axis == dim else 1 for axis in range(len(extent))])
    return loudness


def profile(amount, total, reach, skew):
    portions = [(1 << 20) // math.isqrt(rank ** skew) + 1 for rank in range(2, amount + 1)]
    rest, counts = total - reach - (amount - 1), [1] * (amount - 1)
    while rest > 0:
        candidates = [i for i in range(amount - 1) if counts[i] < reach]
        whole, remaining = sum([portions[i] for i in candidates]), rest
        for i in candidates:
            more = min(reach - counts[i], max(1, remaining * portions[i] // whole), rest)
            counts[i] = counts[i] + more
            rest = rest - more
    return np.array([reach] + counts)


def ragged(rng, amount, total, bound, skew):
    if amount == 2:
        one = jax.random.randint(rng, (), max(1, total - bound), min(bound, total - 1) + 1)
        return jnp.stack([one, total - one])
    tallies = jnp.asarray(profile(amount, total, bound, skew), jnp.int32)
    pairs = (amount - 1) // 2
    donor, taker = tallies[1:1 + 2 * pairs:2], tallies[2:2 + 2 * pairs:2]
    room = jnp.minimum(donor - 1, bound - taker)
    moved = jax.random.randint(jax.random.fold_in(rng, 1), (pairs,), 0, 1 << 20) % (room + 1)
    tallies = tallies.at[1:1 + 2 * pairs:2].set(donor - moved).at[2:2 + 2 * pairs:2].set(taker + moved)
    return tallies[jax.random.permutation(jax.random.fold_in(rng, 2), amount)]


def gaussian(rng, shape, deviation, bound, split=(), dtype=jnp.bfloat16):
    values = jax.random.normal(rng, shape, jnp.float32) * deviation
    if len(split) > 0:
        values = steps_of(rng, shape, split, -0.22, 0.18) * values
    return jnp.clip(values, min=-bound, max=bound).astype(dtype)


def gaussian_with(stream_key, extent, spread, reach, cuts, heavy, dtype=jnp.bfloat16):
    values = spread * jax.random.normal(stream_key, extent, jnp.float32)
    if cuts:
        values = values * steps_of(stream_key, extent, cuts, -0.22, 0.18)
    return jnp.clip(strengthened(values, jax.random.fold_in(stream_key, 3), *heavy), -reach, reach).astype(dtype)


def setup_inputs(seed: int = 0) -> dict:
    splits = jax.random.split(jax.random.key(seed), 16)
    return {
        "tokens": gaussian(splits[0], (TOKENS, D), 1.0, 6.0, ((0, 32), (1, 8))),
        "seg_ids": jnp.searchsorted(jnp.cumsum(ragged(splits[1], REQS, TOKENS, LONG, 1)), jnp.arange(TOKENS), side="right").astype(jnp.int32),
        "w_gate": gaussian(splits[2], (D, INNER), D ** -0.5, 0.125, ((1, 8),)),
        "w_x": gaussian(splits[3], (D, INNER), D ** -0.5, 0.125, ((1, 8),)),
        "w_bc": gaussian(splits[4], (D, 2 * STATE), D ** -0.5, 0.125),
        "w_dt": gaussian(splits[5], (D, HEADS), D ** -0.5, 0.125, ((1, 8),)),
        "conv_x": gaussian(splits[6], (CONV, INNER), 0.5, 3.0, ((1, 8),), jnp.float32),
        "conv_bc": gaussian(splits[7], (CONV, 2 * STATE), 0.5, 3.0, (), jnp.float32),
        "conv_x_bias": gaussian(splits[8], (INNER,), 0.5, 3.0, ((0, 8),), jnp.float32),
        "conv_bc_bias": gaussian(splits[9], (2 * STATE,), 0.5, 3.0, (), jnp.float32),
        "dt_bias": jnp.clip(-4.0 + 3.0 * jax.random.uniform(splits[10], (HEADS,), jnp.float32) ** steps_of(splits[10], (HEADS,), ((0, 8),), -0.2, 0.2), -4.0, -1.0),
        "decay_rate": jnp.clip(jnp.exp(math.log(4.0) - 9.9034876 * jax.random.uniform(splits[11], (HEADS,), jnp.float32) ** steps_of(splits[11], (HEADS,), ((0, 8),), -0.2, 0.2)), 0.0002, 4.0),
        "skip_gain": jnp.clip(0.5 + 1.0 * jax.random.uniform(splits[12], (HEADS,), jnp.float32) ** steps_of(splits[12], (HEADS,), ((0, 8),), -0.2, 0.2), 0.5, 1.5),
        "norm_gain": jnp.clip(1.0 + 0.1 * jax.random.normal(splits[13], (INNER,), jnp.float32), 0.5, 1.5),
        "w_out": gaussian_with(splits[14], (INNER, D), INNER ** -0.5, 0.125, ((0, 8),), (0, 1, 8, 2.0)),
    }


EPSILON = 1e-05
HIGH = lax.Precision.HIGHEST

def conv_mix(projected, weights, offsets, seg_ids):
    total = projected.shape[0]
    values = projected.astype(jnp.float32)
    result = values * weights[0]
    for shift_by in range(1, weights.shape[0]):
        shifted = jnp.concatenate([jnp.zeros((shift_by, values.shape[1]), jnp.float32), values[:total - shift_by]], 0)
        earlier = jnp.concatenate([jnp.full((shift_by,), -1, jnp.int32), seg_ids[:total - shift_by]], 0)
        matches = (earlier == seg_ids)[:, None]
        result = result + jnp.where(matches, shifted, 0.0) * weights[shift_by]
    return result + offsets

def group_step(carry_in, inputs):
    states, prev_id = carry_in
    x_scaled, b_float, c_float, log_decay, idents = inputs
    cumul = jnp.cumsum(log_decay, axis=0)
    places = jnp.arange(idents.shape[0])
    linked = (places[None, :] <= places[:, None]) & (idents[:, None] == idents[None, :])
    gaps = cumul[:, None, :] - cumul[None, :, :]
    decays = jnp.where(linked[:, :, None], jnp.exp(jnp.where(linked[:, :, None], gaps, 0.0)), 0.0)
    scores = jnp.dot(c_float, b_float.T, precision=HIGH)
    within = jnp.einsum('tsh,shp->thp', decays * scores[:, :, None], x_scaled, precision=HIGH)
    enter_weight = jnp.where((idents == prev_id)[:, None], jnp.exp(cumul), 0.0)
    carried = jnp.einsum('tn,hpn->thp', c_float, states, precision=HIGH) * enter_weight[:, :, None]
    tails = jnp.where((idents == idents[-1])[:, None], jnp.exp(cumul[-1][None, :] - cumul), 0.0)
    weighted = x_scaled * tails[:, :, None]
    group_state = jnp.einsum('shp,sn->hpn', weighted, b_float, precision=HIGH)
    passing = jnp.where(idents[-1] == prev_id, jnp.exp(cumul[-1]), 0.0)
    states = passing[:, None, None] * states + group_state
    return ((states, idents[-1]), (within + carried, states))

def reference(tokens, seg_ids, w_gate, w_x, w_bc, w_dt, conv_x, conv_bc, conv_x_bias, conv_bc_bias, dt_bias, decay_rate, skip_gain, norm_gain, w_out):
    total = tokens.shape[0]
    gate_full = jnp.dot(tokens, w_gate, preferred_element_type=jnp.float32)
    x_pre = jnp.dot(tokens, w_x, preferred_element_type=jnp.float32).astype(jnp.bfloat16)
    bc_pre = jnp.dot(tokens, w_bc, preferred_element_type=jnp.float32).astype(jnp.bfloat16)
    dt_raw = jnp.dot(tokens, w_dt, preferred_element_type=jnp.float32)
    x_conv = jax.nn.silu(conv_mix(x_pre, conv_x, conv_x_bias, seg_ids)).astype(jnp.bfloat16)
    bc_conv = jax.nn.silu(conv_mix(bc_pre, conv_bc, conv_bc_bias, seg_ids)).astype(jnp.bfloat16)
    steps_dt = jax.nn.softplus(dt_raw + dt_bias)
    log_decay = -steps_dt * decay_rate
    x_float = x_conv.astype(jnp.float32).reshape(total, HEADS, HEAD_DIM)
    x_scaled = x_float * steps_dt[:, :, None]
    b_float = bc_conv[:, :STATE].astype(jnp.float32)
    c_float = bc_conv[:, STATE:].astype(jnp.float32)
    count = total // GROUP

    def blocks(array):
        return array.reshape((count, GROUP) + array.shape[1:])
    initial = (jnp.zeros((HEADS, HEAD_DIM, STATE), jnp.float32), jnp.array(-1, jnp.int32))
    final_carry, outputs = lax.scan(group_step, initial, (blocks(x_scaled), blocks(b_float), blocks(c_float), blocks(log_decay), blocks(seg_ids)))
    y_groups, group_states = outputs
    ssd_out = y_groups.reshape(total, HEADS, HEAD_DIM) + skip_gain[None, :, None] * x_float
    gated = ssd_out.reshape(total, INNER) * jax.nn.silu(gate_full)
    mean_square = lax.optimization_barrier(jnp.mean(gated * gated, axis=1, keepdims=True))
    hidden = (gated * lax.rsqrt(mean_square + EPSILON) * norm_gain).astype(jnp.bfloat16)
    mixed = jnp.dot(hidden, w_out, preferred_element_type=jnp.float32).astype(jnp.bfloat16)
    per_block = TOK_DEV // GROUP
    end_state = group_states[per_block - 1::per_block]
    return (mixed, end_state)
```

```python
import jax
import jax.numpy as jnp
from jax import lax
from jax.sharding import PartitionSpec as P

GROUP = 256
INNER = 4096


EPSILON = 1e-05
HIGH = lax.Precision.HIGHEST


def shifted(x, axis, by):
    devices = lax.axis_size(axis)
    pairs = [(i, i + by) for i in range(devices) if 0 <= i + by < devices]
    return lax.ppermute(x, axis, pairs)


def carried_in(part, axis, combine, identity):
    place = lax.axis_index(axis)
    gathered = jax.tree.map(lambda a: lax.all_gather(a, axis), part)
    state = jax.tree.map(lambda a, e: jnp.zeros_like(a) + jnp.asarray(e, a.dtype), part, identity)

    def one(hop, state):
        return combine(
            state, jax.tree.map(lambda a: lax.dynamic_index_in_dim(a, hop, 0, False), gathered)
        )

    return lax.fori_loop(0, place, one, state)


def conv_block(projected, edge_rows, weights, offsets, idents, earlier):
    rows_here = projected.shape[0]
    lag_count = edge_rows.shape[0]
    joined = jnp.concatenate([edge_rows, projected], 0).astype(jnp.float32)
    joined_ids = jnp.concatenate([earlier, idents], 0)
    result = joined[lag_count:] * weights[0]
    for shift_by in range(1, lag_count + 1):
        window = joined[lag_count - shift_by : lag_count - shift_by + rows_here]
        matches = joined_ids[lag_count - shift_by : lag_count - shift_by + rows_here] == idents
        result = result + jnp.where(matches[:, None], window, 0.0) * weights[shift_by]
    return result + offsets


def combine(earlier, later):
    return (earlier[0] * later[0], later[0][:, None, None] * earlier[1] + later[1])


def shards(
    tokens,
    seg_ids,
    w_gate,
    w_x,
    w_bc,
    w_dt,
    conv_x,
    conv_bc,
    conv_x_bias,
    conv_bc_bias,
    dt_bias,
    decay_rate,
    skip_gain,
    norm_gain,
    w_out,
):
    rows_here = tokens.shape[0]
    heads_here = w_dt.shape[1]
    inner_here = w_x.shape[1]
    head_width = inner_here // heads_here
    state_width = w_bc.shape[1] // 2
    lag_count = conv_x.shape[0] - 1
    device = lax.axis_index("seq")
    first_row = device * rows_here
    piece = lax.all_gather(tokens, "head", axis=1, tiled=True)

    def partial_product(matrix):
        return jnp.dot(piece, matrix, preferred_element_type=jnp.float32)

    gate_full = partial_product(w_gate)
    x_sum = partial_product(w_x)
    bc_sum = partial_product(w_bc)
    dt_raw = partial_product(w_dt)
    x_pre = x_sum.astype(jnp.bfloat16)
    bc_pre = bc_sum.astype(jnp.bfloat16)
    idents = lax.dynamic_slice_in_dim(seg_ids, first_row, rows_here)
    earlier = lax.dynamic_slice_in_dim(seg_ids, jnp.maximum(first_row - lag_count, 0), lag_count)
    earlier = jnp.where(device > 0, earlier, -1)
    edge_x, edge_bc = shifted(
        (x_pre[rows_here - lag_count :], bc_pre[rows_here - lag_count :]), "seq", 1
    )
    x_conv = jax.nn.silu(conv_block(x_pre, edge_x, conv_x, conv_x_bias, idents, earlier)).astype(
        jnp.bfloat16
    )
    bc_conv = jax.nn.silu(
        conv_block(bc_pre, edge_bc, conv_bc, conv_bc_bias, idents, earlier)
    ).astype(jnp.bfloat16)
    steps_dt = jax.nn.softplus(dt_raw + dt_bias)
    log_decay = -steps_dt * decay_rate
    x_float = x_conv.astype(jnp.float32).reshape(rows_here, heads_here, head_width)
    x_scaled = x_float * steps_dt[:, :, None]
    count = rows_here // GROUP
    group_x = x_scaled.reshape(count, GROUP, heads_here, head_width)
    group_b = bc_conv[:, :state_width].astype(jnp.float32).reshape(count, GROUP, state_width)
    group_c = bc_conv[:, state_width:].astype(jnp.float32).reshape(count, GROUP, state_width)
    group_ids = idents.reshape(count, GROUP)
    cumul = jnp.cumsum(log_decay.reshape(count, GROUP, heads_here), axis=1)
    cumul_heads = jnp.transpose(cumul, (0, 2, 1))
    places = jnp.arange(GROUP)
    causal = places[None, :] <= places[:, None]
    linked = causal[None] & (group_ids[:, :, None] == group_ids[:, None, :])
    gaps = cumul_heads[:, :, :, None] - cumul_heads[:, :, None, :]
    link_heads = linked[:, None, :, :]
    decays = jnp.where(link_heads, jnp.exp(jnp.where(link_heads, gaps, 0.0)), 0.0)
    scores = jnp.einsum("ctn,csn->cts", group_c, group_b, precision=HIGH)
    within = jnp.einsum("chts,cshp->cthp", decays * scores[:, None, :, :], group_x, precision=HIGH)
    last_ids = group_ids[:, -1]
    tails = jnp.where(
        (group_ids == last_ids[:, None])[:, :, None], jnp.exp(cumul[:, -1:, :] - cumul), 0.0
    )
    group_states = jnp.einsum(
        "cshp,csn->chpn", group_x * tails[:, :, :, None], group_b, precision=HIGH
    )
    prior_ids = jnp.concatenate([earlier[-1:], last_ids[:-1]], 0)
    passing = jnp.where((last_ids == prior_ids)[:, None], jnp.exp(cumul[:, -1, :]), 0.0)
    local_list = []
    gain_list = []
    running_state = jnp.zeros((heads_here, head_width, state_width), jnp.float32)
    running_gain = jnp.ones((heads_here,), jnp.float32)
    for group_no in range(count):
        local_list.append(running_state)
        gain_list.append(running_gain)
        running_state = passing[group_no][:, None, None] * running_state + group_states[group_no]
        running_gain = passing[group_no] * running_gain
    blocks_n = lax.axis_size("seq")
    gain_row = jnp.broadcast_to(running_gain[:, None, None], (heads_here, 1, state_width))
    packed = jnp.concatenate([running_state, gain_row], 1)[None]
    gathered = lax.all_gather(packed, "seq", tiled=True)
    all_states = gathered[:, :, :head_width]
    all_gains = gathered[:, :, head_width, 0]
    order = jnp.arange(blocks_n)
    between = (order[:, None] < order[None, :]) & (order[None, :] < device)
    factors = jnp.where(between[:, :, None], all_gains[None, :, :], 1.0)
    weights = jnp.where((order < device)[:, None], jnp.prod(factors, axis=1), 0.0)
    incoming = jnp.einsum("ih,ihpn->hpn", weights, all_states, precision=HIGH)
    entering = jnp.stack(gain_list, 0)[:, :, None, None] * incoming[None] + jnp.stack(local_list, 0)
    enter_weight = jnp.where((group_ids == prior_ids[:, None])[:, :, None], jnp.exp(cumul), 0.0)
    carried = (
        jnp.einsum("ctn,chpn->cthp", group_c, entering, precision=HIGH)
        * enter_weight[:, :, :, None]
    )
    end_state = (running_gain[:, None, None] * incoming + running_state)[None]
    ssd_out = (within + carried).reshape(rows_here, heads_here, head_width) + skip_gain[
        None, :, None
    ] * x_float
    gated = ssd_out.reshape(rows_here, inner_here) * jax.nn.silu(gate_full)
    heads_n = lax.axis_size("head")
    scaled = (gated * norm_gain).astype(jnp.bfloat16)
    partial_out = jnp.dot(scaled, w_out, preferred_element_type=jnp.float32)
    cols = partial_out.shape[1] // heads_n
    square_rows = jnp.sum(gated * gated, axis=1).reshape(-1, cols)
    joined = jnp.concatenate([partial_out, jnp.tile(square_rows, (1, heads_n))], 0)
    summed = lax.psum_scatter(
        joined.astype(jnp.bfloat16), "head", scatter_dimension=1, tiled=True
    ).astype(jnp.float32)
    mean_square = (summed[rows_here:].reshape(rows_here) / INNER)[:, None]
    mixed = (summed[:rows_here] * lax.rsqrt(mean_square + EPSILON)).astype(jnp.bfloat16)
    return (mixed, end_state)


def solution(mesh):
    return jax.shard_map(
        shards,
        mesh=mesh,
        in_specs=(
            P("seq", "head"),
            P(),
            P(None, "head"),
            P(None, "head"),
            P(),
            P(None, "head"),
            P(None, "head"),
            P(),
            P("head"),
            P(),
            P("head"),
            P("head"),
            P("head"),
            P("head"),
            P("head", None),
        ),
        out_specs=(P("seq", "head"), P("seq", "head", None, None)),
        check_vma=False,
    )
```

```python
import jax
import jax.numpy as jnp
from jax import lax
from jax.sharding import PartitionSpec as P

GROUP = 256
INNER = 4096


EPSILON = 1e-05
HIGH = lax.Precision.HIGHEST


def shifted(x, axis, by):
    devices = lax.axis_size(axis)
    pairs = [(i, i + by) for i in range(devices) if 0 <= i + by < devices]
    return lax.ppermute(x, axis, pairs)


def carried_in(part, axis, combine, identity):
    place = lax.axis_index(axis)
    gathered = jax.tree.map(lambda a: lax.all_gather(a, axis), part)
    state = jax.tree.map(lambda a, e: jnp.zeros_like(a) + jnp.asarray(e, a.dtype), part, identity)

    def one(hop, state):
        return combine(
            state, jax.tree.map(lambda a: lax.dynamic_index_in_dim(a, hop, 0, False), gathered)
        )

    return lax.fori_loop(0, place, one, state)


def conv_block(projected, edge_rows, weights, offsets, idents, earlier):
    rows_here = projected.shape[0]
    lag_count = edge_rows.shape[0]
    joined = jnp.concatenate([edge_rows, projected], 0).astype(jnp.float32)
    joined_ids = jnp.concatenate([earlier, idents], 0)
    result = joined[lag_count:] * weights[0]
    for shift_by in range(1, lag_count + 1):
        window = joined[lag_count - shift_by : lag_count - shift_by + rows_here]
        matches = joined_ids[lag_count - shift_by : lag_count - shift_by + rows_here] == idents
        result = result + jnp.where(matches[:, None], window, 0.0) * weights[shift_by]
    return result + offsets


def combine(earlier, later):
    return (earlier[0] * later[0], later[0][:, None, None] * earlier[1] + later[1])


def shards(
    tokens,
    seg_ids,
    w_gate,
    w_x,
    w_bc,
    w_dt,
    conv_x,
    conv_bc,
    conv_x_bias,
    conv_bc_bias,
    dt_bias,
    decay_rate,
    skip_gain,
    norm_gain,
    w_out,
):
    rows_here = tokens.shape[0]
    heads_here = w_dt.shape[1]
    inner_here = w_x.shape[1]
    head_width = inner_here // heads_here
    state_width = w_bc.shape[1] // 2
    lag_count = conv_x.shape[0] - 1
    device = lax.axis_index("seq")
    first_row = device * rows_here
    piece = lax.all_gather(tokens, "head", axis=1, tiled=True)

    def partial_product(matrix):
        return jnp.dot(piece, matrix, preferred_element_type=jnp.float32)

    gate_full = partial_product(w_gate)
    x_sum = partial_product(w_x)
    bc_sum = partial_product(w_bc)
    dt_raw = partial_product(w_dt)
    x_pre = x_sum.astype(jnp.bfloat16)
    bc_pre = bc_sum.astype(jnp.bfloat16)
    idents = lax.dynamic_slice_in_dim(seg_ids, first_row, rows_here)
    earlier = lax.dynamic_slice_in_dim(seg_ids, jnp.maximum(first_row - lag_count, 0), lag_count)
    earlier = jnp.where(device > 0, earlier, -1)
    edge_x, edge_bc = shifted(
        (x_pre[rows_here - lag_count :], bc_pre[rows_here - lag_count :]), "seq", 1
    )
    x_conv = jax.nn.silu(conv_block(x_pre, edge_x, conv_x, conv_x_bias, idents, earlier)).astype(
        jnp.bfloat16
    )
    bc_conv = jax.nn.silu(
        conv_block(bc_pre, edge_bc, conv_bc, conv_bc_bias, idents, earlier)
    ).astype(jnp.bfloat16)
    steps_dt = jax.nn.softplus(dt_raw + dt_bias)
    log_decay = -steps_dt * decay_rate
    x_float = x_conv.astype(jnp.float32).reshape(rows_here, heads_here, head_width)
    x_scaled = x_float * steps_dt[:, :, None]
    count = rows_here // GROUP
    group_x = x_scaled.reshape(count, GROUP, heads_here, head_width)
    group_b = bc_conv[:, :state_width].astype(jnp.float32).reshape(count, GROUP, state_width)
    group_c = bc_conv[:, state_width:].astype(jnp.float32).reshape(count, GROUP, state_width)
    group_ids = idents.reshape(count, GROUP)
    cumul = jnp.cumsum(log_decay.reshape(count, GROUP, heads_here), axis=1)
    cumul_heads = jnp.transpose(cumul, (0, 2, 1))
    places = jnp.arange(GROUP)
    causal = places[None, :] <= places[:, None]
    linked = causal[None] & (group_ids[:, :, None] == group_ids[:, None, :])
    gaps = cumul_heads[:, :, :, None] - cumul_heads[:, :, None, :]
    link_heads = linked[:, None, :, :]
    decays = jnp.where(link_heads, jnp.exp(jnp.where(link_heads, gaps, 0.0)), 0.0)
    scores = jnp.einsum("ctn,csn->cts", group_c, group_b, precision=HIGH)
    within = jnp.einsum("chts,cshp->cthp", decays * scores[:, None, :, :], group_x, precision=HIGH)
    last_ids = group_ids[:, -1]
    tails = jnp.where(
        (group_ids == last_ids[:, None])[:, :, None], jnp.exp(cumul[:, -1:, :] - cumul), 0.0
    )
    group_states = jnp.einsum(
        "cshp,csn->chpn", group_x * tails[:, :, :, None], group_b, precision=HIGH
    )
    prior_ids = jnp.concatenate([earlier[-1:], last_ids[:-1]], 0)
    passing = jnp.where((last_ids == prior_ids)[:, None], jnp.exp(cumul[:, -1, :]), 0.0)
    local_list = []
    gain_list = []
    running_state = jnp.zeros((heads_here, head_width, state_width), jnp.float32)
    running_gain = jnp.ones((heads_here,), jnp.float32)
    for group_no in range(count):
        local_list.append(running_state)
        gain_list.append(running_gain)
        running_state = passing[group_no][:, None, None] * running_state + group_states[group_no]
        running_gain = passing[group_no] * running_gain
    blocks_n = lax.axis_size("seq")
    gain_row = jnp.broadcast_to(running_gain[:, None, None], (heads_here, 1, state_width))
    packed = jnp.concatenate([running_state, gain_row], 1)
    prefix = shifted(packed, "seq", 1)
    prefix = jnp.where(device > 0, prefix, jnp.concatenate([0.0 * running_state, 1.0 + 0.0 * gain_row], 1))
    reach = 1
    while reach < blocks_n:
        earlier_part = shifted(prefix, "seq", reach)
        later_gain = prefix[:, head_width:, :]
        joined_part = jnp.concatenate(
            [
                later_gain * earlier_part[:, :head_width, :] + prefix[:, :head_width, :],
                later_gain * earlier_part[:, head_width:, :],
            ],
            1,
        )
        prefix = jnp.where(device >= reach, joined_part, prefix)
        reach *= 2
    incoming = prefix[:, :head_width, :]
    entering = jnp.stack(gain_list, 0)[:, :, None, None] * incoming[None] + jnp.stack(local_list, 0)
    enter_weight = jnp.where((group_ids == prior_ids[:, None])[:, :, None], jnp.exp(cumul), 0.0)
    carried = (
        jnp.einsum("ctn,chpn->cthp", group_c, entering, precision=HIGH)
        * enter_weight[:, :, :, None]
    )
    end_state = (running_gain[:, None, None] * incoming + running_state)[None]
    ssd_out = (within + carried).reshape(rows_here, heads_here, head_width) + skip_gain[
        None, :, None
    ] * x_float
    gated = ssd_out.reshape(rows_here, inner_here) * jax.nn.silu(gate_full)
    heads_n = lax.axis_size("head")
    scaled = (gated * norm_gain).astype(jnp.bfloat16)
    partial_out = jnp.dot(scaled, w_out, preferred_element_type=jnp.float32)
    cols = partial_out.shape[1] // heads_n
    square_rows = jnp.sum(gated * gated, axis=1).reshape(-1, cols)
    joined = jnp.concatenate([partial_out, jnp.tile(square_rows, (1, heads_n))], 0)
    summed = lax.psum_scatter(
        joined.astype(jnp.bfloat16), "head", scatter_dimension=1, tiled=True
    ).astype(jnp.float32)
    mean_square = (summed[rows_here:].reshape(rows_here) / INNER)[:, None]
    mixed = (summed[:rows_here] * lax.rsqrt(mean_square + EPSILON)).astype(jnp.bfloat16)
    return (mixed, end_state)


def solution(mesh):
    return jax.shard_map(
        shards,
        mesh=mesh,
        in_specs=(
            P("seq", "head"),
            P(),
            P(None, "head"),
            P(None, "head"),
            P(),
            P(None, "head"),
            P(None, "head"),
            P(),
            P("head"),
            P(),
            P("head"),
            P("head"),
            P("head"),
            P("head"),
            P("head", None),
        ),
        out_specs=(P("seq", "head"), P("seq", "head", None, None)),
        check_vma=False,
    )
```

```python
import jax
import jax.numpy as jnp
from jax import lax
from jax.sharding import PartitionSpec as P

GROUP = 256
INNER = 4096
LONG = 16384


EPSILON = 1e-05
HIGH = lax.Precision.HIGHEST


def shifted(x, axis, by):
    devices = lax.axis_size(axis)
    pairs = [(i, i + by) for i in range(devices) if 0 <= i + by < devices]
    return lax.ppermute(x, axis, pairs)


def carried_in(part, axis, combine, identity):
    place = lax.axis_index(axis)
    gathered = jax.tree.map(lambda a: lax.all_gather(a, axis), part)
    state = jax.tree.map(lambda a, e: jnp.zeros_like(a) + jnp.asarray(e, a.dtype), part, identity)

    def one(hop, state):
        return combine(
            state, jax.tree.map(lambda a: lax.dynamic_index_in_dim(a, hop, 0, False), gathered)
        )

    return lax.fori_loop(0, place, one, state)


def conv_block(projected, edge_rows, weights, offsets, idents, earlier):
    rows_here = projected.shape[0]
    lag_count = edge_rows.shape[0]
    joined = jnp.concatenate([edge_rows, projected], 0).astype(jnp.float32)
    joined_ids = jnp.concatenate([earlier, idents], 0)
    result = joined[lag_count:] * weights[0]
    for shift_by in range(1, lag_count + 1):
        window = joined[lag_count - shift_by : lag_count - shift_by + rows_here]
        matches = joined_ids[lag_count - shift_by : lag_count - shift_by + rows_here] == idents
        result = result + jnp.where(matches[:, None], window, 0.0) * weights[shift_by]
    return result + offsets


def combine(earlier, later):
    return (earlier[0] * later[0], later[0][:, None, None] * earlier[1] + later[1])


def shards(
    tokens,
    seg_ids,
    w_gate,
    w_x,
    w_bc,
    w_dt,
    conv_x,
    conv_bc,
    conv_x_bias,
    conv_bc_bias,
    dt_bias,
    decay_rate,
    skip_gain,
    norm_gain,
    w_out,
):
    rows_here = tokens.shape[0]
    heads_here = w_dt.shape[1]
    inner_here = w_x.shape[1]
    head_width = inner_here // heads_here
    state_width = w_bc.shape[1] // 2
    lag_count = conv_x.shape[0] - 1
    device = lax.axis_index("seq")
    first_row = device * rows_here
    piece = lax.all_gather(tokens, "head", axis=1, tiled=True)

    def partial_product(matrix):
        return jnp.dot(piece, matrix, preferred_element_type=jnp.float32)

    gate_full = partial_product(w_gate)
    x_sum = partial_product(w_x)
    bc_sum = partial_product(w_bc)
    dt_raw = partial_product(w_dt)
    x_pre = x_sum.astype(jnp.bfloat16)
    bc_pre = bc_sum.astype(jnp.bfloat16)
    idents = lax.dynamic_slice_in_dim(seg_ids, first_row, rows_here)
    earlier = lax.dynamic_slice_in_dim(seg_ids, jnp.maximum(first_row - lag_count, 0), lag_count)
    earlier = jnp.where(device > 0, earlier, -1)
    edge_x, edge_bc = shifted(
        (x_pre[rows_here - lag_count :], bc_pre[rows_here - lag_count :]), "seq", 1
    )
    x_conv = jax.nn.silu(conv_block(x_pre, edge_x, conv_x, conv_x_bias, idents, earlier)).astype(
        jnp.bfloat16
    )
    bc_conv = jax.nn.silu(
        conv_block(bc_pre, edge_bc, conv_bc, conv_bc_bias, idents, earlier)
    ).astype(jnp.bfloat16)
    steps_dt = jax.nn.softplus(dt_raw + dt_bias)
    log_decay = -steps_dt * decay_rate
    x_float = x_conv.astype(jnp.float32).reshape(rows_here, heads_here, head_width)
    x_scaled = x_float * steps_dt[:, :, None]
    count = rows_here // GROUP
    group_x = x_scaled.reshape(count, GROUP, heads_here, head_width)
    group_b = bc_conv[:, :state_width].astype(jnp.float32).reshape(count, GROUP, state_width)
    group_c = bc_conv[:, state_width:].astype(jnp.float32).reshape(count, GROUP, state_width)
    group_ids = idents.reshape(count, GROUP)
    cumul = jnp.cumsum(log_decay.reshape(count, GROUP, heads_here), axis=1)
    cumul_heads = jnp.transpose(cumul, (0, 2, 1))
    places = jnp.arange(GROUP)
    causal = places[None, :] <= places[:, None]
    linked = causal[None] & (group_ids[:, :, None] == group_ids[:, None, :])
    gaps = cumul_heads[:, :, :, None] - cumul_heads[:, :, None, :]
    link_heads = linked[:, None, :, :]
    decays = jnp.where(link_heads, jnp.exp(jnp.where(link_heads, gaps, 0.0)), 0.0)
    scores = jnp.einsum("ctn,csn->cts", group_c, group_b, precision=HIGH)
    within = jnp.einsum("chts,cshp->cthp", decays * scores[:, None, :, :], group_x, precision=HIGH)
    last_ids = group_ids[:, -1]
    tails = jnp.where(
        (group_ids == last_ids[:, None])[:, :, None], jnp.exp(cumul[:, -1:, :] - cumul), 0.0
    )
    group_states = jnp.einsum(
        "cshp,csn->chpn", group_x * tails[:, :, :, None], group_b, precision=HIGH
    )
    prior_ids = jnp.concatenate([earlier[-1:], last_ids[:-1]], 0)
    passing = jnp.where((last_ids == prior_ids)[:, None], jnp.exp(cumul[:, -1, :]), 0.0)
    local_list = []
    gain_list = []
    running_state = jnp.zeros((heads_here, head_width, state_width), jnp.float32)
    running_gain = jnp.ones((heads_here,), jnp.float32)
    for group_no in range(count):
        local_list.append(running_state)
        gain_list.append(running_gain)
        running_state = passing[group_no][:, None, None] * running_state + group_states[group_no]
        running_gain = passing[group_no] * running_gain
    blocks_n = lax.axis_size("seq")
    gain_row = jnp.broadcast_to(running_gain[:, None, None], (heads_here, 1, state_width))
    packed = jnp.concatenate([running_state, gain_row], 1)
    prefix = shifted(packed, "seq", 1)
    prefix = jnp.where(device > 0, prefix, jnp.concatenate([0.0 * running_state, 1.0 + 0.0 * gain_row], 1))
    reach = 1
    while reach < min(blocks_n, LONG // rows_here):
        earlier_part = shifted(prefix, "seq", reach)
        later_gain = prefix[:, head_width:, :]
        joined_part = jnp.concatenate(
            [
                later_gain * earlier_part[:, :head_width, :] + prefix[:, :head_width, :],
                later_gain * earlier_part[:, head_width:, :],
            ],
            1,
        )
        prefix = jnp.where(device >= reach, joined_part, prefix)
        reach *= 2
    incoming = prefix[:, :head_width, :]
    entering = jnp.stack(gain_list, 0)[:, :, None, None] * incoming[None] + jnp.stack(local_list, 0)
    enter_weight = jnp.where((group_ids == prior_ids[:, None])[:, :, None], jnp.exp(cumul), 0.0)
    carried = (
        jnp.einsum("ctn,chpn->cthp", group_c, entering, precision=HIGH)
        * enter_weight[:, :, :, None]
    )
    end_state = (running_gain[:, None, None] * incoming + running_state)[None]
    ssd_out = (within + carried).reshape(rows_here, heads_here, head_width) + skip_gain[
        None, :, None
    ] * x_float
    heads_n = lax.axis_size("head")
    halves = 2
    span = rows_here // halves
    mixed_parts = []
    for half in range(halves):
        rows = slice(half * span, (half + 1) * span)
        gated = ssd_out.reshape(rows_here, inner_here)[rows] * jax.nn.silu(gate_full[rows])
        scaled = (gated * norm_gain).astype(jnp.bfloat16)
        partial_out = jnp.dot(scaled, w_out, preferred_element_type=jnp.float32)
        cols = partial_out.shape[1] // heads_n
        square_rows = jnp.sum(gated * gated, axis=1).reshape(-1, cols)
        joined = jnp.concatenate([partial_out, jnp.tile(square_rows, (1, heads_n))], 0)
        summed = lax.psum_scatter(
            joined.astype(jnp.bfloat16), "head", scatter_dimension=1, tiled=True
        ).astype(jnp.float32)
        mean_square = (summed[span:].reshape(span) / INNER)[:, None]
        mixed_parts.append((summed[:span] * lax.rsqrt(mean_square + EPSILON)).astype(jnp.bfloat16))
    mixed = jnp.concatenate(mixed_parts, 0)
    return (mixed, end_state)


def solution(mesh):
    return jax.shard_map(
        shards,
        mesh=mesh,
        in_specs=(
            P("seq", "head"),
            P(),
            P(None, "head"),
            P(None, "head"),
            P(),
            P(None, "head"),
            P(None, "head"),
            P(),
            P("head"),
            P(),
            P("head"),
            P("head"),
            P("head"),
            P("head"),
            P("head", None),
        ),
        out_specs=(P("seq", "head"), P("seq", "head", None, None)),
        check_vma=False,
    )
```

```python
import jax
import jax.numpy as jnp
from jax import lax
from jax.sharding import PartitionSpec as P

GROUP = 256
INNER = 4096
LONG = 16384


EPSILON = 1e-05
HIGH = lax.Precision.HIGHEST


def shifted(x, axis, by):
    devices = lax.axis_size(axis)
    pairs = [(i, i + by) for i in range(devices) if 0 <= i + by < devices]
    return lax.ppermute(x, axis, pairs)


def carried_in(part, axis, combine, identity):
    place = lax.axis_index(axis)
    gathered = jax.tree.map(lambda a: lax.all_gather(a, axis), part)
    state = jax.tree.map(lambda a, e: jnp.zeros_like(a) + jnp.asarray(e, a.dtype), part, identity)

    def one(hop, state):
        return combine(
            state, jax.tree.map(lambda a: lax.dynamic_index_in_dim(a, hop, 0, False), gathered)
        )

    return lax.fori_loop(0, place, one, state)


def conv_block(projected, edge_rows, weights, offsets, idents, earlier):
    rows_here = projected.shape[0]
    lag_count = edge_rows.shape[0]
    joined = jnp.concatenate([edge_rows, projected], 0).astype(jnp.float32)
    joined_ids = jnp.concatenate([earlier, idents], 0)
    result = joined[lag_count:] * weights[0]
    for shift_by in range(1, lag_count + 1):
        window = joined[lag_count - shift_by : lag_count - shift_by + rows_here]
        matches = joined_ids[lag_count - shift_by : lag_count - shift_by + rows_here] == idents
        result = result + jnp.where(matches[:, None], window, 0.0) * weights[shift_by]
    return result + offsets


def combine(earlier, later):
    return (earlier[0] * later[0], later[0][:, None, None] * earlier[1] + later[1])


def shards(
    tokens,
    seg_ids,
    w_gate,
    w_x,
    w_bc,
    w_dt,
    conv_x,
    conv_bc,
    conv_x_bias,
    conv_bc_bias,
    dt_bias,
    decay_rate,
    skip_gain,
    norm_gain,
    w_out,
):
    rows_here = tokens.shape[0]
    heads_here = w_dt.shape[1]
    inner_here = w_x.shape[1]
    head_width = inner_here // heads_here
    state_width = w_bc.shape[1] // 2
    lag_count = conv_x.shape[0] - 1
    device = lax.axis_index("seq")
    first_row = device * rows_here
    piece = lax.all_gather(tokens, "head", axis=1, tiled=True)

    def partial_product(matrix):
        return jnp.dot(piece, matrix, preferred_element_type=jnp.float32)

    gate_full = partial_product(w_gate)
    x_sum = partial_product(w_x)
    bc_sum = partial_product(w_bc)
    dt_raw = partial_product(w_dt)
    x_pre = x_sum.astype(jnp.bfloat16)
    bc_pre = bc_sum.astype(jnp.bfloat16)
    idents = lax.dynamic_slice_in_dim(seg_ids, first_row, rows_here)
    earlier = lax.dynamic_slice_in_dim(seg_ids, jnp.maximum(first_row - lag_count, 0), lag_count)
    earlier = jnp.where(device > 0, earlier, -1)
    edge_x, edge_bc = shifted(
        (x_pre[rows_here - lag_count :], bc_pre[rows_here - lag_count :]), "seq", 1
    )
    x_conv = jax.nn.silu(conv_block(x_pre, edge_x, conv_x, conv_x_bias, idents, earlier)).astype(
        jnp.bfloat16
    )
    bc_conv = jax.nn.silu(
        conv_block(bc_pre, edge_bc, conv_bc, conv_bc_bias, idents, earlier)
    ).astype(jnp.bfloat16)
    steps_dt = jax.nn.softplus(dt_raw + dt_bias)
    log_decay = -steps_dt * decay_rate
    x_float = x_conv.astype(jnp.float32).reshape(rows_here, heads_here, head_width)
    x_scaled = x_float * steps_dt[:, :, None]
    count = rows_here // GROUP
    group_x = x_scaled.reshape(count, GROUP, heads_here, head_width)
    group_b = bc_conv[:, :state_width].astype(jnp.float32).reshape(count, GROUP, state_width)
    group_c = bc_conv[:, state_width:].astype(jnp.float32).reshape(count, GROUP, state_width)
    group_ids = idents.reshape(count, GROUP)
    cumul = jnp.cumsum(log_decay.reshape(count, GROUP, heads_here), axis=1)
    cumul_heads = jnp.transpose(cumul, (0, 2, 1))
    places = jnp.arange(GROUP)
    causal = places[None, :] <= places[:, None]
    linked = causal[None] & (group_ids[:, :, None] == group_ids[:, None, :])
    gaps = cumul_heads[:, :, :, None] - cumul_heads[:, :, None, :]
    link_heads = linked[:, None, :, :]
    decays = jnp.where(link_heads, jnp.exp(jnp.where(link_heads, gaps, 0.0)), 0.0)
    scores = jnp.einsum("ctn,csn->cts", group_c, group_b, precision=HIGH)
    within = jnp.einsum("chts,cshp->cthp", decays * scores[:, None, :, :], group_x, precision=HIGH)
    last_ids = group_ids[:, -1]
    tails = jnp.where(
        (group_ids == last_ids[:, None])[:, :, None], jnp.exp(cumul[:, -1:, :] - cumul), 0.0
    )
    group_states = jnp.einsum(
        "cshp,csn->chpn", group_x * tails[:, :, :, None], group_b, precision=HIGH
    )
    prior_ids = jnp.concatenate([earlier[-1:], last_ids[:-1]], 0)
    passing = jnp.where((last_ids == prior_ids)[:, None], jnp.exp(cumul[:, -1, :]), 0.0)
    local_list = []
    gain_list = []
    running_state = jnp.zeros((heads_here, head_width, state_width), jnp.float32)
    running_gain = jnp.ones((heads_here,), jnp.float32)
    for group_no in range(count):
        local_list.append(running_state)
        gain_list.append(running_gain)
        running_state = passing[group_no][:, None, None] * running_state + group_states[group_no]
        running_gain = passing[group_no] * running_gain
    blocks_n = lax.axis_size("seq")
    gain_row = jnp.broadcast_to(running_gain[:, None, None], (heads_here, 1, state_width))
    packed = jnp.concatenate([running_state, gain_row], 1)
    identity = jnp.concatenate([0.0 * running_state, 1.0 + 0.0 * gain_row], 1)

    def joined_of(earlier_part, later_part):
        later_gain = later_part[:, head_width:, :]
        return jnp.concatenate(
            [
                later_gain * earlier_part[:, :head_width, :] + later_part[:, :head_width, :],
                later_gain * earlier_part[:, head_width:, :],
            ],
            1,
        )

    def fetched(part, by):
        return jnp.where(device >= by, shifted(part, "seq", by), identity)

    depth = min(blocks_n, LONG // rows_here)
    span = 1
    while span * span < depth:
        span += 1
    recent = identity
    for by in range(span, 0, -1):
        if by < blocks_n:
            recent = joined_of(recent, fetched(packed, by))
    prefix = recent
    for hop in range(1, (depth + span - 1) // span):
        if hop * span < blocks_n:
            prefix = joined_of(fetched(recent, hop * span), prefix)
    incoming = prefix[:, :head_width, :]
    entering = jnp.stack(gain_list, 0)[:, :, None, None] * incoming[None] + jnp.stack(local_list, 0)
    enter_weight = jnp.where((group_ids == prior_ids[:, None])[:, :, None], jnp.exp(cumul), 0.0)
    carried = (
        jnp.einsum("ctn,chpn->cthp", group_c, entering, precision=HIGH)
        * enter_weight[:, :, :, None]
    )
    end_state = (running_gain[:, None, None] * incoming + running_state)[None]
    ssd_out = (within + carried).reshape(rows_here, heads_here, head_width) + skip_gain[
        None, :, None
    ] * x_float
    heads_n = lax.axis_size("head")
    gated = ssd_out.reshape(rows_here, inner_here) * jax.nn.silu(gate_full)
    scaled = (gated * norm_gain).astype(jnp.bfloat16)
    partial_out = jnp.dot(scaled, w_out, preferred_element_type=jnp.float32)
    cols = partial_out.shape[1] // heads_n
    square_rows = jnp.sum(gated * gated, axis=1).reshape(-1, cols)
    joined = jnp.concatenate([partial_out, jnp.tile(square_rows, (1, heads_n))], 0)
    summed = lax.psum_scatter(
        joined.astype(jnp.bfloat16), "head", scatter_dimension=1, tiled=True
    ).astype(jnp.float32)
    mean_square = (summed[rows_here:].reshape(rows_here) / INNER)[:, None]
    mixed = (summed[:rows_here] * lax.rsqrt(mean_square + EPSILON)).astype(jnp.bfloat16)
    return (mixed, end_state)


def solution(mesh):
    return jax.shard_map(
        shards,
        mesh=mesh,
        in_specs=(
            P("seq", "head"),
            P(),
            P(None, "head"),
            P(None, "head"),
            P(),
            P(None, "head"),
            P(None, "head"),
            P(),
            P("head"),
            P(),
            P("head"),
            P("head"),
            P("head"),
            P("head"),
            P("head", None),
        ),
        out_specs=(P("seq", "head"), P("seq", "head", None, None)),
        check_vma=False,
    )
```

```python
import jax
import jax.numpy as jnp
from jax import lax
from jax.sharding import PartitionSpec as P

GROUP = 256
INNER = 4096
LONG = 16384


EPSILON = 1e-05
HIGH = lax.Precision.HIGHEST


def shifted(x, axis, by):
    devices = lax.axis_size(axis)
    pairs = [(i, i + by) for i in range(devices) if 0 <= i + by < devices]
    return lax.ppermute(x, axis, pairs)


def carried_in(part, axis, combine, identity):
    place = lax.axis_index(axis)
    gathered = jax.tree.map(lambda a: lax.all_gather(a, axis), part)
    state = jax.tree.map(lambda a, e: jnp.zeros_like(a) + jnp.asarray(e, a.dtype), part, identity)

    def one(hop, state):
        return combine(
            state, jax.tree.map(lambda a: lax.dynamic_index_in_dim(a, hop, 0, False), gathered)
        )

    return lax.fori_loop(0, place, one, state)


def conv_block(projected, edge_rows, weights, offsets, idents, earlier):
    rows_here = projected.shape[0]
    lag_count = edge_rows.shape[0]
    joined = jnp.concatenate([edge_rows, projected], 0).astype(jnp.float32)
    joined_ids = jnp.concatenate([earlier, idents], 0)
    result = joined[lag_count:] * weights[0]
    for shift_by in range(1, lag_count + 1):
        window = joined[lag_count - shift_by : lag_count - shift_by + rows_here]
        matches = joined_ids[lag_count - shift_by : lag_count - shift_by + rows_here] == idents
        result = result + jnp.where(matches[:, None], window, 0.0) * weights[shift_by]
    return result + offsets


def combine(earlier, later):
    return (earlier[0] * later[0], later[0][:, None, None] * earlier[1] + later[1])


def shards(
    tokens,
    seg_ids,
    w_gate,
    w_x,
    w_bc,
    w_dt,
    conv_x,
    conv_bc,
    conv_x_bias,
    conv_bc_bias,
    dt_bias,
    decay_rate,
    skip_gain,
    norm_gain,
    w_out,
):
    rows_here = tokens.shape[0]
    heads_here = w_dt.shape[1]
    inner_here = w_x.shape[1]
    head_width = inner_here // heads_here
    state_width = w_bc.shape[1] // 2
    lag_count = conv_x.shape[0] - 1
    device = lax.axis_index("seq")
    first_row = device * rows_here
    piece = lax.all_gather(tokens, "head", axis=1, tiled=True)

    def partial_product(matrix):
        return jnp.dot(piece, matrix, preferred_element_type=jnp.float32)

    gate_full = partial_product(w_gate)
    x_sum = partial_product(w_x)
    bc_sum = partial_product(w_bc)
    dt_raw = partial_product(w_dt)
    x_pre = x_sum.astype(jnp.bfloat16)
    bc_pre = bc_sum.astype(jnp.bfloat16)
    idents = lax.dynamic_slice_in_dim(seg_ids, first_row, rows_here)
    earlier = lax.dynamic_slice_in_dim(seg_ids, jnp.maximum(first_row - lag_count, 0), lag_count)
    earlier = jnp.where(device > 0, earlier, -1)
    edge_x, edge_bc = shifted(
        (x_pre[rows_here - lag_count :], bc_pre[rows_here - lag_count :]), "seq", 1
    )
    x_conv = jax.nn.silu(conv_block(x_pre, edge_x, conv_x, conv_x_bias, idents, earlier)).astype(
        jnp.bfloat16
    )
    bc_conv = jax.nn.silu(
        conv_block(bc_pre, edge_bc, conv_bc, conv_bc_bias, idents, earlier)
    ).astype(jnp.bfloat16)
    steps_dt = jax.nn.softplus(dt_raw + dt_bias)
    log_decay = -steps_dt * decay_rate
    x_float = x_conv.astype(jnp.float32).reshape(rows_here, heads_here, head_width)
    x_scaled = x_float * steps_dt[:, :, None]
    count = rows_here // GROUP
    group_x = x_scaled.reshape(count, GROUP, heads_here, head_width)
    group_b = bc_conv[:, :state_width].astype(jnp.float32).reshape(count, GROUP, state_width)
    group_c = bc_conv[:, state_width:].astype(jnp.float32).reshape(count, GROUP, state_width)
    group_ids = idents.reshape(count, GROUP)
    cumul = jnp.cumsum(log_decay.reshape(count, GROUP, heads_here), axis=1)
    cumul_heads = jnp.transpose(cumul, (0, 2, 1))
    places = jnp.arange(GROUP)
    causal = places[None, :] <= places[:, None]
    linked = causal[None] & (group_ids[:, :, None] == group_ids[:, None, :])
    gaps = cumul_heads[:, :, :, None] - cumul_heads[:, :, None, :]
    link_heads = linked[:, None, :, :]
    decays = jnp.where(link_heads, jnp.exp(jnp.where(link_heads, gaps, 0.0)), 0.0)
    scores = jnp.einsum("ctn,csn->cts", group_c, group_b, precision=HIGH)
    within = jnp.einsum("chts,cshp->cthp", decays * scores[:, None, :, :], group_x, precision=HIGH)
    last_ids = group_ids[:, -1]
    tails = jnp.where(
        (group_ids == last_ids[:, None])[:, :, None], jnp.exp(cumul[:, -1:, :] - cumul), 0.0
    )
    group_states = jnp.einsum(
        "cshp,csn->chpn", group_x * tails[:, :, :, None], group_b, precision=HIGH
    )
    prior_ids = jnp.concatenate([earlier[-1:], last_ids[:-1]], 0)
    passing = jnp.where((last_ids == prior_ids)[:, None], jnp.exp(cumul[:, -1, :]), 0.0)
    local_list = []
    gain_list = []
    running_state = jnp.zeros((heads_here, head_width, state_width), jnp.float32)
    running_gain = jnp.ones((heads_here,), jnp.float32)
    for group_no in range(count):
        local_list.append(running_state)
        gain_list.append(running_gain)
        running_state = passing[group_no][:, None, None] * running_state + group_states[group_no]
        running_gain = passing[group_no] * running_gain
    blocks_n = lax.axis_size("seq")
    gain_row = jnp.broadcast_to(running_gain[:, None, None], (heads_here, 1, state_width))
    packed = jnp.concatenate([running_state, gain_row], 1)
    identity = jnp.concatenate([0.0 * running_state, 1.0 + 0.0 * gain_row], 1)

    def joined_of(earlier_part, later_part):
        later_gain = later_part[:, head_width:, :]
        return jnp.concatenate(
            [
                later_gain * earlier_part[:, :head_width, :] + later_part[:, :head_width, :],
                later_gain * earlier_part[:, head_width:, :],
            ],
            1,
        )

    def fetched(part, by):
        return jnp.where(device >= by, shifted(part, "seq", by), identity)

    depth = min(blocks_n, LONG // rows_here)
    span = 1
    while span * span < depth:
        span += 1
    recent = identity
    for by in range(span, 0, -1):
        if by < blocks_n:
            recent = joined_of(recent, fetched(packed, by))
    prefix = recent
    for hop in range(1, (depth + span - 1) // span):
        if hop * span < blocks_n:
            prefix = joined_of(fetched(recent, hop * span), prefix)
    incoming = prefix[:, :head_width, :]
    entering = jnp.stack(gain_list, 0)[:, :, None, None] * incoming[None] + jnp.stack(local_list, 0)
    enter_weight = jnp.where((group_ids == prior_ids[:, None])[:, :, None], jnp.exp(cumul), 0.0)
    carried = (
        jnp.einsum("ctn,chpn->cthp", group_c, entering, precision=HIGH)
        * enter_weight[:, :, :, None]
    )
    end_state = (running_gain[:, None, None] * incoming + running_state)[None]
    heads_n = lax.axis_size("head")
    group_shape = (count, GROUP, heads_here, head_width)
    gate_act = jax.nn.silu(gate_full).reshape(group_shape)
    direct = skip_gain[:, None] * x_float.reshape(group_shape)
    gated = (within + carried + direct) * gate_act
    scaled = (gated * norm_gain.reshape(heads_here, head_width)).astype(jnp.bfloat16)
    partial_out = jnp.einsum(
        "cthp,hpo->cto",
        scaled,
        w_out.reshape(heads_here, head_width, w_out.shape[1]),
        preferred_element_type=jnp.float32,
    ).reshape(rows_here, w_out.shape[1])
    cols = partial_out.shape[1] // heads_n
    square_rows = jnp.sum(gated * gated, axis=(2, 3)).reshape(-1, cols)
    joined = jnp.concatenate([partial_out, jnp.tile(square_rows, (1, heads_n))], 0)
    summed = lax.psum_scatter(
        joined.astype(jnp.bfloat16), "head", scatter_dimension=1, tiled=True
    ).astype(jnp.float32)
    mean_square = (summed[rows_here:].reshape(rows_here) / INNER)[:, None]
    mixed = (summed[:rows_here] * lax.rsqrt(mean_square + EPSILON)).astype(jnp.bfloat16)
    return (mixed, end_state)


def solution(mesh):
    return jax.shard_map(
        shards,
        mesh=mesh,
        in_specs=(
            P("seq", "head"),
            P(),
            P(None, "head"),
            P(None, "head"),
            P(),
            P(None, "head"),
            P(None, "head"),
            P(),
            P("head"),
            P(),
            P("head"),
            P("head"),
            P("head"),
            P("head"),
            P("head", None),
        ),
        out_specs=(P("seq", "head"), P("seq", "head", None, None)),
        check_vma=False,
    )
```

```python
import jax
import jax.numpy as jnp
from jax import lax
from jax.sharding import PartitionSpec as P

GROUP = 256
INNER = 4096
LONG = 16384


EPSILON = 1e-05
HIGH = lax.Precision.HIGHEST


def shifted(x, axis, by):
    devices = lax.axis_size(axis)
    pairs = [(i, i + by) for i in range(devices) if 0 <= i + by < devices]
    return lax.ppermute(x, axis, pairs)


def carried_in(part, axis, combine, identity):
    place = lax.axis_index(axis)
    gathered = jax.tree.map(lambda a: lax.all_gather(a, axis), part)
    state = jax.tree.map(lambda a, e: jnp.zeros_like(a) + jnp.asarray(e, a.dtype), part, identity)

    def one(hop, state):
        return combine(
            state, jax.tree.map(lambda a: lax.dynamic_index_in_dim(a, hop, 0, False), gathered)
        )

    return lax.fori_loop(0, place, one, state)


def conv_block(projected, edge_rows, weights, offsets, idents, earlier):
    rows_here = projected.shape[0]
    lag_count = edge_rows.shape[0]
    joined = jnp.concatenate([edge_rows, projected], 0).astype(jnp.float32)
    joined_ids = jnp.concatenate([earlier, idents], 0)
    result = joined[lag_count:] * weights[0]
    for shift_by in range(1, lag_count + 1):
        window = joined[lag_count - shift_by : lag_count - shift_by + rows_here]
        matches = joined_ids[lag_count - shift_by : lag_count - shift_by + rows_here] == idents
        result = result + jnp.where(matches[:, None], window, 0.0) * weights[shift_by]
    return result + offsets


def combine(earlier, later):
    return (earlier[0] * later[0], later[0][:, None, None] * earlier[1] + later[1])


def shards(
    tokens,
    seg_ids,
    w_gate,
    w_x,
    w_bc,
    w_dt,
    conv_x,
    conv_bc,
    conv_x_bias,
    conv_bc_bias,
    dt_bias,
    decay_rate,
    skip_gain,
    norm_gain,
    w_out,
):
    rows_here = tokens.shape[0]
    heads_here = w_dt.shape[1]
    inner_here = w_x.shape[1]
    head_width = inner_here // heads_here
    state_width = w_bc.shape[1] // 2
    lag_count = conv_x.shape[0] - 1
    device = lax.axis_index("seq")
    first_row = device * rows_here
    piece = lax.all_gather(tokens, "head", axis=1, tiled=True)

    def partial_product(matrix):
        return jnp.dot(piece, matrix, preferred_element_type=jnp.float32)

    x_sum = partial_product(w_x)
    bc_sum = partial_product(w_bc)
    dt_raw = partial_product(w_dt)
    x_pre = x_sum.astype(jnp.bfloat16)
    bc_pre = bc_sum.astype(jnp.bfloat16)
    idents = lax.dynamic_slice_in_dim(seg_ids, first_row, rows_here)
    earlier = lax.dynamic_slice_in_dim(seg_ids, jnp.maximum(first_row - lag_count, 0), lag_count)
    earlier = jnp.where(device > 0, earlier, -1)
    edges = shifted(
        jnp.concatenate([x_pre[rows_here - lag_count :], bc_pre[rows_here - lag_count :]], 1),
        "seq",
        1,
    )
    edge_x, edge_bc = edges[:, :inner_here], edges[:, inner_here:]
    x_conv = jax.nn.silu(conv_block(x_pre, edge_x, conv_x, conv_x_bias, idents, earlier)).astype(
        jnp.bfloat16
    )
    bc_conv = jax.nn.silu(
        conv_block(bc_pre, edge_bc, conv_bc, conv_bc_bias, idents, earlier)
    ).astype(jnp.bfloat16)
    steps_dt = jax.nn.softplus(dt_raw + dt_bias)
    log_decay = -steps_dt * decay_rate
    x_float = x_conv.astype(jnp.float32).reshape(rows_here, heads_here, head_width)
    x_scaled = x_float * steps_dt[:, :, None]
    count = rows_here // GROUP
    group_x = x_scaled.reshape(count, GROUP, heads_here, head_width)
    group_b = bc_conv[:, :state_width].astype(jnp.float32).reshape(count, GROUP, state_width)
    group_c = bc_conv[:, state_width:].astype(jnp.float32).reshape(count, GROUP, state_width)
    group_ids = idents.reshape(count, GROUP)
    cumul = jnp.cumsum(log_decay.reshape(count, GROUP, heads_here), axis=1)
    cumul_heads = jnp.transpose(cumul, (0, 2, 1))
    places = jnp.arange(GROUP)
    causal = places[None, :] <= places[:, None]
    linked = causal[None] & (group_ids[:, :, None] == group_ids[:, None, :])
    gaps = cumul_heads[:, :, :, None] - cumul_heads[:, :, None, :]
    link_heads = linked[:, None, :, :]
    decays = jnp.where(link_heads, jnp.exp(jnp.where(link_heads, gaps, 0.0)), 0.0)
    scores = jnp.einsum("ctn,csn->cts", group_c, group_b, precision=HIGH)
    within = jnp.einsum("chts,cshp->cthp", decays * scores[:, None, :, :], group_x, precision=HIGH)
    last_ids = group_ids[:, -1]
    tails = jnp.where(
        (group_ids == last_ids[:, None])[:, :, None], jnp.exp(cumul[:, -1:, :] - cumul), 0.0
    )
    group_states = jnp.einsum(
        "cshp,csn->chpn", group_x * tails[:, :, :, None], group_b, precision=HIGH
    )
    prior_ids = jnp.concatenate([earlier[-1:], last_ids[:-1]], 0)
    passing = jnp.where((last_ids == prior_ids)[:, None], jnp.exp(cumul[:, -1, :]), 0.0)
    local_list = []
    gain_list = []
    running_state = jnp.zeros((heads_here, head_width, state_width), jnp.float32)
    running_gain = jnp.ones((heads_here,), jnp.float32)
    for group_no in range(count):
        local_list.append(running_state)
        gain_list.append(running_gain)
        running_state = passing[group_no][:, None, None] * running_state + group_states[group_no]
        running_gain = passing[group_no] * running_gain
    blocks_n = lax.axis_size("seq")
    gain_row = jnp.broadcast_to(running_gain[:, None, None], (heads_here, 1, state_width))
    packed = jnp.concatenate([running_state, gain_row], 1)
    identity = jnp.concatenate([0.0 * running_state, 1.0 + 0.0 * gain_row], 1)
    late_piece, packed = lax.optimization_barrier((piece, packed))
    gate_full = jnp.dot(late_piece, w_gate, preferred_element_type=jnp.float32)

    def joined_of(earlier_part, later_part):
        later_gain = later_part[:, head_width:, :]
        return jnp.concatenate(
            [
                later_gain * earlier_part[:, :head_width, :] + later_part[:, :head_width, :],
                later_gain * earlier_part[:, head_width:, :],
            ],
            1,
        )

    def fetched(part, by):
        return jnp.where(device >= by, shifted(part, "seq", by), identity)

    depth = min(blocks_n, LONG // rows_here)
    span = 1
    while span * span < depth:
        span += 1
    recent = identity
    for by in range(span, 0, -1):
        if by < blocks_n:
            recent = joined_of(recent, fetched(packed, by))
    prefix = recent
    for hop in range(1, (depth + span - 1) // span):
        if hop * span < blocks_n:
            prefix = joined_of(fetched(recent, hop * span), prefix)
    incoming = prefix[:, :head_width, :]
    entering = jnp.stack(gain_list, 0)[:, :, None, None] * incoming[None] + jnp.stack(local_list, 0)
    enter_weight = jnp.where((group_ids == prior_ids[:, None])[:, :, None], jnp.exp(cumul), 0.0)
    carried = (
        jnp.einsum("ctn,chpn->cthp", group_c, entering, precision=HIGH)
        * enter_weight[:, :, :, None]
    )
    end_state = (running_gain[:, None, None] * incoming + running_state)[None]
    heads_n = lax.axis_size("head")
    group_shape = (count, GROUP, heads_here, head_width)
    gate_act = jax.nn.silu(gate_full).reshape(group_shape)
    direct = skip_gain[:, None] * x_float.reshape(group_shape)
    gated = (within + carried + direct) * gate_act
    scaled = (gated * norm_gain.reshape(heads_here, head_width)).astype(jnp.bfloat16)
    partial_out = jnp.einsum(
        "cthp,hpo->cto",
        scaled,
        w_out.reshape(heads_here, head_width, w_out.shape[1]),
        preferred_element_type=jnp.float32,
    ).reshape(rows_here, w_out.shape[1])
    cols = partial_out.shape[1] // heads_n
    square_rows = jnp.sum(gated * gated, axis=(2, 3)).reshape(-1, cols)
    joined = jnp.concatenate([partial_out, jnp.tile(square_rows, (1, heads_n))], 0)
    summed = lax.psum_scatter(
        joined.astype(jnp.bfloat16), "head", scatter_dimension=1, tiled=True
    ).astype(jnp.float32)
    mean_square = (summed[rows_here:].reshape(rows_here) / INNER)[:, None]
    mixed = (summed[:rows_here] * lax.rsqrt(mean_square + EPSILON)).astype(jnp.bfloat16)
    return (mixed, end_state)


def solution(mesh):
    return jax.shard_map(
        shards,
        mesh=mesh,
        in_specs=(
            P("seq", "head"),
            P(),
            P(None, "head"),
            P(None, "head"),
            P(),
            P(None, "head"),
            P(None, "head"),
            P(),
            P("head"),
            P(),
            P("head"),
            P("head"),
            P("head"),
            P("head"),
            P("head", None),
        ),
        out_specs=(P("seq", "head"), P("seq", "head", None, None)),
        check_vma=False,
    )
```

```python
import jax
import jax.numpy as jnp
from jax import lax
from jax.sharding import PartitionSpec as P

GROUP = 256
INNER = 4096
LONG = 16384


EPSILON = 1e-05
HIGH = lax.Precision.HIGHEST


def shifted(x, axis, by):
    devices = lax.axis_size(axis)
    pairs = [(i, i + by) for i in range(devices) if 0 <= i + by < devices]
    return lax.ppermute(x, axis, pairs)


def carried_in(part, axis, combine, identity):
    place = lax.axis_index(axis)
    gathered = jax.tree.map(lambda a: lax.all_gather(a, axis), part)
    state = jax.tree.map(lambda a, e: jnp.zeros_like(a) + jnp.asarray(e, a.dtype), part, identity)

    def one(hop, state):
        return combine(
            state, jax.tree.map(lambda a: lax.dynamic_index_in_dim(a, hop, 0, False), gathered)
        )

    return lax.fori_loop(0, place, one, state)


def conv_block(projected, edge_rows, weights, offsets, idents, earlier):
    rows_here = projected.shape[0]
    lag_count = edge_rows.shape[0]
    joined = jnp.concatenate([edge_rows, projected], 0).astype(jnp.float32)
    joined_ids = jnp.concatenate([earlier, idents], 0)
    result = joined[lag_count:] * weights[0]
    for shift_by in range(1, lag_count + 1):
        window = joined[lag_count - shift_by : lag_count - shift_by + rows_here]
        matches = joined_ids[lag_count - shift_by : lag_count - shift_by + rows_here] == idents
        result = result + jnp.where(matches[:, None], window, 0.0) * weights[shift_by]
    return result + offsets


def combine(earlier, later):
    return (earlier[0] * later[0], later[0][:, None, None] * earlier[1] + later[1])


def shards(
    tokens,
    seg_ids,
    w_gate,
    w_x,
    w_bc,
    w_dt,
    conv_x,
    conv_bc,
    conv_x_bias,
    conv_bc_bias,
    dt_bias,
    decay_rate,
    skip_gain,
    norm_gain,
    w_out,
):
    rows_here = tokens.shape[0]
    heads_here = w_dt.shape[1]
    inner_here = w_x.shape[1]
    head_width = inner_here // heads_here
    state_width = w_bc.shape[1] // 2
    lag_count = conv_x.shape[0] - 1
    device = lax.axis_index("seq")
    first_row = device * rows_here
    piece = lax.all_gather(tokens, "head", axis=1, tiled=True)

    def partial_product(matrix):
        return jnp.dot(piece, matrix, preferred_element_type=jnp.float32)

    x_sum = partial_product(w_x)
    bc_sum = partial_product(w_bc)
    dt_raw = partial_product(w_dt)
    x_pre = x_sum.astype(jnp.bfloat16)
    bc_pre = bc_sum.astype(jnp.bfloat16)
    idents = lax.dynamic_slice_in_dim(seg_ids, first_row, rows_here)
    earlier = lax.dynamic_slice_in_dim(seg_ids, jnp.maximum(first_row - lag_count, 0), lag_count)
    earlier = jnp.where(device > 0, earlier, -1)
    edges = shifted(
        jnp.concatenate([x_pre[rows_here - lag_count :], bc_pre[rows_here - lag_count :]], 1),
        "seq",
        1,
    )
    edge_x, edge_bc = edges[:, :inner_here], edges[:, inner_here:]
    x_conv = jax.nn.silu(conv_block(x_pre, edge_x, conv_x, conv_x_bias, idents, earlier)).astype(
        jnp.bfloat16
    )
    bc_conv = jax.nn.silu(
        conv_block(bc_pre, edge_bc, conv_bc, conv_bc_bias, idents, earlier)
    ).astype(jnp.bfloat16)
    steps_dt = jax.nn.softplus(dt_raw + dt_bias)
    log_decay = -steps_dt * decay_rate
    x_float = x_conv.astype(jnp.float32).reshape(rows_here, heads_here, head_width)
    x_scaled = x_float * steps_dt[:, :, None]
    count = rows_here // GROUP
    group_x = x_scaled.reshape(count, GROUP, heads_here, head_width)
    group_b = bc_conv[:, :state_width].astype(jnp.float32).reshape(count, GROUP, state_width)
    group_c = bc_conv[:, state_width:].astype(jnp.float32).reshape(count, GROUP, state_width)
    group_ids = idents.reshape(count, GROUP)
    cumul = jnp.cumsum(log_decay.reshape(count, GROUP, heads_here), axis=1)
    cumul_heads = jnp.transpose(cumul, (0, 2, 1))
    places = jnp.arange(GROUP)
    causal = places[None, :] <= places[:, None]
    linked = causal[None] & (group_ids[:, :, None] == group_ids[:, None, :])
    gaps = cumul_heads[:, :, :, None] - cumul_heads[:, :, None, :]
    link_heads = linked[:, None, :, :]
    decays = jnp.where(link_heads, jnp.exp(jnp.where(link_heads, gaps, 0.0)), 0.0)
    scores = jnp.einsum("ctn,csn->cts", group_c, group_b, precision=HIGH)
    within = jnp.einsum("chts,cshp->cthp", decays * scores[:, None, :, :], group_x, precision=HIGH)
    last_ids = group_ids[:, -1]
    tails = jnp.where(
        (group_ids == last_ids[:, None])[:, :, None], jnp.exp(cumul[:, -1:, :] - cumul), 0.0
    )
    group_states = jnp.einsum(
        "cshp,csn->chpn", group_x * tails[:, :, :, None], group_b, precision=HIGH
    )
    prior_ids = jnp.concatenate([earlier[-1:], last_ids[:-1]], 0)
    passing = jnp.where((last_ids == prior_ids)[:, None], jnp.exp(cumul[:, -1, :]), 0.0)
    local_list = []
    gain_list = []
    running_state = jnp.zeros((heads_here, head_width, state_width), jnp.float32)
    running_gain = jnp.ones((heads_here,), jnp.float32)
    for group_no in range(count):
        local_list.append(running_state)
        gain_list.append(running_gain)
        running_state = passing[group_no][:, None, None] * running_state + group_states[group_no]
        running_gain = passing[group_no] * running_gain
    blocks_n = lax.axis_size("seq")
    gain_row = jnp.broadcast_to(running_gain[:, None, None], (heads_here, 1, state_width))
    packed = jnp.concatenate([running_state, gain_row], 1)
    identity = jnp.concatenate([0.0 * running_state, 1.0 + 0.0 * gain_row], 1)
    late_piece, packed = lax.optimization_barrier((piece, packed))
    gate_turned = jnp.einsum(
        "ctd,dk->ckt",
        late_piece.reshape(rows_here // GROUP, GROUP, late_piece.shape[1]),
        w_gate,
        preferred_element_type=jnp.float32,
    )

    def joined_of(earlier_part, later_part):
        later_gain = later_part[:, head_width:, :]
        return jnp.concatenate(
            [
                later_gain * earlier_part[:, :head_width, :] + later_part[:, :head_width, :],
                later_gain * earlier_part[:, head_width:, :],
            ],
            1,
        )

    def fetched(part, by):
        return jnp.where(device >= by, shifted(part, "seq", by), identity)

    depth = min(blocks_n, LONG // rows_here)
    span = 1
    while span * span < depth:
        span += 1
    recent = identity
    for by in range(span, 0, -1):
        if by < blocks_n:
            recent = joined_of(recent, fetched(packed, by))
    prefix = recent
    for hop in range(1, (depth + span - 1) // span):
        if hop * span < blocks_n:
            prefix = joined_of(fetched(recent, hop * span), prefix)
    incoming = prefix[:, :head_width, :]
    entering = jnp.stack(gain_list, 0)[:, :, None, None] * incoming[None] + jnp.stack(local_list, 0)
    enter_weight = jnp.where((group_ids == prior_ids[:, None])[:, :, None], jnp.exp(cumul), 0.0)
    carried = (
        jnp.einsum("ctn,chpn->cthp", group_c, entering, precision=HIGH)
        * enter_weight[:, :, :, None]
    )
    end_state = (running_gain[:, None, None] * incoming + running_state)[None]
    heads_n = lax.axis_size("head")
    group_shape = (count, GROUP, heads_here, head_width)
    gate_act = jnp.transpose(
        jax.nn.silu(gate_turned).reshape(count, heads_here, head_width, GROUP), (0, 3, 1, 2)
    )
    direct = skip_gain[:, None] * x_float.reshape(group_shape)
    gated = (within + carried + direct) * gate_act
    scaled = (gated * norm_gain.reshape(heads_here, head_width)).astype(jnp.bfloat16)
    partial_out = jnp.einsum(
        "cthp,hpo->cto",
        scaled,
        w_out.reshape(heads_here, head_width, w_out.shape[1]),
        preferred_element_type=jnp.float32,
    ).reshape(rows_here, w_out.shape[1])
    cols = partial_out.shape[1] // heads_n
    square_rows = jnp.sum(gated * gated, axis=(2, 3)).reshape(-1, cols)
    joined = jnp.concatenate([partial_out, jnp.tile(square_rows, (1, heads_n))], 0)
    summed = lax.psum_scatter(
        joined.astype(jnp.bfloat16), "head", scatter_dimension=1, tiled=True
    ).astype(jnp.float32)
    mean_square = (summed[rows_here:].reshape(rows_here) / INNER)[:, None]
    mixed = (summed[:rows_here] * lax.rsqrt(mean_square + EPSILON)).astype(jnp.bfloat16)
    return (mixed, end_state)


def solution(mesh):
    return jax.shard_map(
        shards,
        mesh=mesh,
        in_specs=(
            P("seq", "head"),
            P(),
            P(None, "head"),
            P(None, "head"),
            P(),
            P(None, "head"),
            P(None, "head"),
            P(),
            P("head"),
            P(),
            P("head"),
            P("head"),
            P("head"),
            P("head"),
            P("head", None),
        ),
        out_specs=(P("seq", "head"), P("seq", "head", None, None)),
        check_vma=False,
    )
```

```python
import jax
import jax.numpy as jnp
from jax import lax
from jax.sharding import PartitionSpec as P

GROUP = 256
INNER = 4096
LONG = 16384


EPSILON = 1e-05
HIGH = lax.Precision.HIGHEST


def shifted(x, axis, by):
    devices = lax.axis_size(axis)
    pairs = [(i, i + by) for i in range(devices) if 0 <= i + by < devices]
    return lax.ppermute(x, axis, pairs)


def carried_in(part, axis, combine, identity):
    place = lax.axis_index(axis)
    gathered = jax.tree.map(lambda a: lax.all_gather(a, axis), part)
    state = jax.tree.map(lambda a, e: jnp.zeros_like(a) + jnp.asarray(e, a.dtype), part, identity)

    def one(hop, state):
        return combine(
            state, jax.tree.map(lambda a: lax.dynamic_index_in_dim(a, hop, 0, False), gathered)
        )

    return lax.fori_loop(0, place, one, state)


def conv_block(projected, edge_rows, weights, offsets, idents, earlier):
    rows_here = projected.shape[0]
    lag_count = edge_rows.shape[0]
    joined = jnp.concatenate([edge_rows, projected], 0).astype(jnp.float32)
    joined_ids = jnp.concatenate([earlier, idents], 0)
    result = joined[lag_count:] * weights[0]
    for shift_by in range(1, lag_count + 1):
        window = joined[lag_count - shift_by : lag_count - shift_by + rows_here]
        matches = joined_ids[lag_count - shift_by : lag_count - shift_by + rows_here] == idents
        result = result + jnp.where(matches[:, None], window, 0.0) * weights[shift_by]
    return result + offsets


def combine(earlier, later):
    return (earlier[0] * later[0], later[0][:, None, None] * earlier[1] + later[1])


def shards(
    tokens,
    seg_ids,
    w_gate,
    w_x,
    w_bc,
    w_dt,
    conv_x,
    conv_bc,
    conv_x_bias,
    conv_bc_bias,
    dt_bias,
    decay_rate,
    skip_gain,
    norm_gain,
    w_out,
):
    rows_here = tokens.shape[0]
    heads_here = w_dt.shape[1]
    inner_here = w_x.shape[1]
    head_width = inner_here // heads_here
    state_width = w_bc.shape[1] // 2
    lag_count = conv_x.shape[0] - 1
    device = lax.axis_index("seq")
    first_row = device * rows_here
    piece = lax.all_gather(tokens, "head", axis=1, tiled=True)

    def partial_product(matrix):
        return jnp.dot(piece, matrix, preferred_element_type=jnp.float32)

    x_sum = partial_product(w_x)
    bc_sum = partial_product(w_bc)
    dt_raw = partial_product(w_dt)
    x_pre = x_sum.astype(jnp.bfloat16)
    bc_pre = bc_sum.astype(jnp.bfloat16)
    idents = lax.dynamic_slice_in_dim(seg_ids, first_row, rows_here)
    earlier = lax.dynamic_slice_in_dim(seg_ids, jnp.maximum(first_row - lag_count, 0), lag_count)
    earlier = jnp.where(device > 0, earlier, -1)
    edges = shifted(
        jnp.concatenate([x_pre[rows_here - lag_count :], bc_pre[rows_here - lag_count :]], 1),
        "seq",
        1,
    )
    edge_x, edge_bc = edges[:, :inner_here], edges[:, inner_here:]
    x_conv = jax.nn.silu(conv_block(x_pre, edge_x, conv_x, conv_x_bias, idents, earlier)).astype(
        jnp.bfloat16
    )
    bc_conv = jax.nn.silu(
        conv_block(bc_pre, edge_bc, conv_bc, conv_bc_bias, idents, earlier)
    ).astype(jnp.bfloat16)
    steps_dt = jax.nn.softplus(dt_raw + dt_bias)
    log_decay = -steps_dt * decay_rate
    x_float = x_conv.astype(jnp.float32).reshape(rows_here, heads_here, head_width)
    x_scaled = x_float * steps_dt[:, :, None]
    count = rows_here // GROUP
    group_x = x_scaled.reshape(count, GROUP, heads_here, head_width)
    group_b = bc_conv[:, :state_width].astype(jnp.float32).reshape(count, GROUP, state_width)
    group_c = bc_conv[:, state_width:].astype(jnp.float32).reshape(count, GROUP, state_width)
    group_ids = idents.reshape(count, GROUP)
    cumul = jnp.cumsum(log_decay.reshape(count, GROUP, heads_here), axis=1)
    cumul_heads = jnp.transpose(cumul, (0, 2, 1))
    places = jnp.arange(GROUP)
    causal = places[None, :] <= places[:, None]
    linked = causal[None] & (group_ids[:, :, None] == group_ids[:, None, :])
    gaps = cumul_heads[:, :, :, None] - cumul_heads[:, :, None, :]
    link_heads = linked[:, None, :, :]
    decays = jnp.where(link_heads, jnp.exp(jnp.where(link_heads, gaps, 0.0)), 0.0)
    scores = jnp.einsum("ctn,csn->cts", group_c, group_b, precision=HIGH)
    within = jnp.einsum("chts,cshp->cthp", decays * scores[:, None, :, :], group_x, precision=HIGH)
    last_ids = group_ids[:, -1]
    tails = jnp.where(
        (group_ids == last_ids[:, None])[:, :, None], jnp.exp(cumul[:, -1:, :] - cumul), 0.0
    )
    group_states = jnp.einsum(
        "cshp,csn->chpn", group_x * tails[:, :, :, None], group_b, precision=HIGH
    )
    prior_ids = jnp.concatenate([earlier[-1:], last_ids[:-1]], 0)
    passing = jnp.where((last_ids == prior_ids)[:, None], jnp.exp(cumul[:, -1, :]), 0.0)
    local_list = []
    gain_list = []
    running_state = jnp.zeros((heads_here, head_width, state_width), jnp.float32)
    running_gain = jnp.ones((heads_here,), jnp.float32)
    for group_no in range(count):
        local_list.append(running_state)
        gain_list.append(running_gain)
        running_state = passing[group_no][:, None, None] * running_state + group_states[group_no]
        running_gain = passing[group_no] * running_gain
    blocks_n = lax.axis_size("seq")
    gain_row = jnp.broadcast_to(running_gain[:, None, None], (heads_here, 1, state_width))
    packed = jnp.concatenate([running_state, gain_row], 1)
    identity = jnp.concatenate([0.0 * running_state, 1.0 + 0.0 * gain_row], 1)
    late_piece, packed = lax.optimization_barrier((piece, packed))
    gate_turned = jnp.stack(
        [
            jnp.dot(
                w_gate.T,
                late_piece[group_no * GROUP : (group_no + 1) * GROUP].T,
                preferred_element_type=jnp.float32,
            )
            for group_no in range(rows_here // GROUP)
        ],
        0,
    )

    def joined_of(earlier_part, later_part):
        later_gain = later_part[:, head_width:, :]
        return jnp.concatenate(
            [
                later_gain * earlier_part[:, :head_width, :] + later_part[:, :head_width, :],
                later_gain * earlier_part[:, head_width:, :],
            ],
            1,
        )

    def fetched(part, by):
        return jnp.where(device >= by, shifted(part, "seq", by), identity)

    depth = min(blocks_n, LONG // rows_here)
    span = 1
    while span * span < depth:
        span += 1
    recent = identity
    for by in range(span, 0, -1):
        if by < blocks_n:
            recent = joined_of(recent, fetched(packed, by))
    prefix = recent
    for hop in range(1, (depth + span - 1) // span):
        if hop * span < blocks_n:
            prefix = joined_of(fetched(recent, hop * span), prefix)
    incoming = prefix[:, :head_width, :]
    entering = jnp.stack(gain_list, 0)[:, :, None, None] * incoming[None] + jnp.stack(local_list, 0)
    enter_weight = jnp.where((group_ids == prior_ids[:, None])[:, :, None], jnp.exp(cumul), 0.0)
    carried = (
        jnp.einsum("ctn,chpn->cthp", group_c, entering, precision=HIGH)
        * enter_weight[:, :, :, None]
    )
    end_state = (running_gain[:, None, None] * incoming + running_state)[None]
    heads_n = lax.axis_size("head")
    group_shape = (count, GROUP, heads_here, head_width)
    gate_act = jnp.transpose(
        jax.nn.silu(gate_turned).reshape(count, heads_here, head_width, GROUP), (0, 3, 1, 2)
    )
    direct = skip_gain[:, None] * x_float.reshape(group_shape)
    gated = (within + carried + direct) * gate_act
    scaled = (gated * norm_gain.reshape(heads_here, head_width)).astype(jnp.bfloat16)
    partial_out = jnp.einsum(
        "cthp,hpo->cto",
        scaled,
        w_out.reshape(heads_here, head_width, w_out.shape[1]),
        preferred_element_type=jnp.float32,
    ).reshape(rows_here, w_out.shape[1])
    cols = partial_out.shape[1] // heads_n
    square_rows = jnp.sum(gated * gated, axis=(2, 3)).reshape(-1, cols)
    joined = jnp.concatenate([partial_out, jnp.tile(square_rows, (1, heads_n))], 0)
    summed = lax.psum_scatter(
        joined.astype(jnp.bfloat16), "head", scatter_dimension=1, tiled=True
    ).astype(jnp.float32)
    mean_square = (summed[rows_here:].reshape(rows_here) / INNER)[:, None]
    mixed = (summed[:rows_here] * lax.rsqrt(mean_square + EPSILON)).astype(jnp.bfloat16)
    return (mixed, end_state)


def solution(mesh):
    return jax.shard_map(
        shards,
        mesh=mesh,
        in_specs=(
            P("seq", "head"),
            P(),
            P(None, "head"),
            P(None, "head"),
            P(),
            P(None, "head"),
            P(None, "head"),
            P(),
            P("head"),
            P(),
            P("head"),
            P("head"),
            P("head"),
            P("head"),
            P("head", None),
        ),
        out_specs=(P("seq", "head"), P("seq", "head", None, None)),
        check_vma=False,
    )
```

```python
import jax
import jax.numpy as jnp
from jax import lax
from jax.sharding import PartitionSpec as P

GROUP = 256
INNER = 4096
LONG = 16384


EPSILON = 1e-05
HIGH = lax.Precision.HIGHEST


def shifted(x, axis, by):
    devices = lax.axis_size(axis)
    pairs = [(i, i + by) for i in range(devices) if 0 <= i + by < devices]
    return lax.ppermute(x, axis, pairs)


def carried_in(part, axis, combine, identity):
    place = lax.axis_index(axis)
    gathered = jax.tree.map(lambda a: lax.all_gather(a, axis), part)
    state = jax.tree.map(lambda a, e: jnp.zeros_like(a) + jnp.asarray(e, a.dtype), part, identity)

    def one(hop, state):
        return combine(
            state, jax.tree.map(lambda a: lax.dynamic_index_in_dim(a, hop, 0, False), gathered)
        )

    return lax.fori_loop(0, place, one, state)


def conv_block(projected, edge_rows, weights, offsets, idents, earlier):
    rows_here = projected.shape[0]
    lag_count = edge_rows.shape[0]
    joined = jnp.concatenate([edge_rows, projected], 0).astype(jnp.float32)
    joined_ids = jnp.concatenate([earlier, idents], 0)
    result = joined[lag_count:] * weights[0]
    for shift_by in range(1, lag_count + 1):
        window = joined[lag_count - shift_by : lag_count - shift_by + rows_here]
        matches = joined_ids[lag_count - shift_by : lag_count - shift_by + rows_here] == idents
        result = result + jnp.where(matches[:, None], window, 0.0) * weights[shift_by]
    return result + offsets


def conv_turned(projected, edge_rows, weights, offsets, idents, earlier):
    rows_here = projected.shape[1]
    lag_count = edge_rows.shape[0]
    joined = jnp.concatenate([edge_rows.T, projected], 1).astype(jnp.float32)
    joined_ids = jnp.concatenate([earlier, idents], 0)
    result = joined[:, lag_count:] * weights[0][:, None]
    for shift_by in range(1, lag_count + 1):
        window = joined[:, lag_count - shift_by : lag_count - shift_by + rows_here]
        matches = joined_ids[lag_count - shift_by : lag_count - shift_by + rows_here] == idents
        result = result + jnp.where(matches[None, :], window, 0.0) * weights[shift_by][:, None]
    return result + offsets[:, None]


def combine(earlier, later):
    return (earlier[0] * later[0], later[0][:, None, None] * earlier[1] + later[1])


def shards(
    tokens,
    seg_ids,
    w_gate,
    w_x,
    w_bc,
    w_dt,
    conv_x,
    conv_bc,
    conv_x_bias,
    conv_bc_bias,
    dt_bias,
    decay_rate,
    skip_gain,
    norm_gain,
    w_out,
):
    rows_here = tokens.shape[0]
    heads_here = w_dt.shape[1]
    inner_here = w_x.shape[1]
    head_width = inner_here // heads_here
    state_width = w_bc.shape[1] // 2
    lag_count = conv_x.shape[0] - 1
    device = lax.axis_index("seq")
    first_row = device * rows_here
    piece = lax.all_gather(tokens, "head", axis=1, tiled=True)

    def partial_product(matrix):
        return jnp.dot(piece, matrix, preferred_element_type=jnp.float32)

    x_turned = jnp.dot(w_x.T, piece.T, preferred_element_type=jnp.float32).astype(jnp.bfloat16)
    bc_sum = partial_product(w_bc)
    dt_raw = partial_product(w_dt)
    bc_pre = bc_sum.astype(jnp.bfloat16)
    idents = lax.dynamic_slice_in_dim(seg_ids, first_row, rows_here)
    earlier = lax.dynamic_slice_in_dim(seg_ids, jnp.maximum(first_row - lag_count, 0), lag_count)
    earlier = jnp.where(device > 0, earlier, -1)
    edges = shifted(
        jnp.concatenate([x_turned[:, rows_here - lag_count :].T, bc_pre[rows_here - lag_count :]], 1),
        "seq",
        1,
    )
    edge_x, edge_bc = edges[:, :inner_here], edges[:, inner_here:]
    x_conv = jax.nn.silu(
        conv_turned(x_turned, edge_x, conv_x, conv_x_bias, idents, earlier)
    ).astype(jnp.bfloat16)
    bc_conv = jax.nn.silu(
        conv_block(bc_pre, edge_bc, conv_bc, conv_bc_bias, idents, earlier)
    ).astype(jnp.bfloat16)
    steps_dt = jax.nn.softplus(dt_raw + dt_bias)
    log_decay = -steps_dt * decay_rate
    x_float = x_conv.astype(jnp.float32).reshape(heads_here, head_width, rows_here)
    x_scaled = x_float * steps_dt.T[:, None, :]
    count = rows_here // GROUP
    group_x = jnp.transpose(x_scaled.reshape(heads_here, head_width, count, GROUP), (2, 3, 0, 1))
    group_b = bc_conv[:, :state_width].astype(jnp.float32).reshape(count, GROUP, state_width)
    group_c = bc_conv[:, state_width:].astype(jnp.float32).reshape(count, GROUP, state_width)
    group_ids = idents.reshape(count, GROUP)
    cumul = jnp.cumsum(log_decay.reshape(count, GROUP, heads_here), axis=1)
    cumul_heads = jnp.transpose(cumul, (0, 2, 1))
    places = jnp.arange(GROUP)
    causal = places[None, :] <= places[:, None]
    linked = causal[None] & (group_ids[:, :, None] == group_ids[:, None, :])
    gaps = cumul_heads[:, :, :, None] - cumul_heads[:, :, None, :]
    link_heads = linked[:, None, :, :]
    decays = jnp.where(link_heads, jnp.exp(jnp.where(link_heads, gaps, 0.0)), 0.0)
    scores = jnp.einsum("ctn,csn->cts", group_c, group_b, precision=HIGH)
    within = jnp.einsum("chts,cshp->cthp", decays * scores[:, None, :, :], group_x, precision=HIGH)
    last_ids = group_ids[:, -1]
    tails = jnp.where(
        (group_ids == last_ids[:, None])[:, :, None], jnp.exp(cumul[:, -1:, :] - cumul), 0.0
    )
    group_states = jnp.einsum(
        "cshp,csn->chpn", group_x * tails[:, :, :, None], group_b, precision=HIGH
    )
    prior_ids = jnp.concatenate([earlier[-1:], last_ids[:-1]], 0)
    passing = jnp.where((last_ids == prior_ids)[:, None], jnp.exp(cumul[:, -1, :]), 0.0)
    local_list = []
    gain_list = []
    running_state = jnp.zeros((heads_here, head_width, state_width), jnp.float32)
    running_gain = jnp.ones((heads_here,), jnp.float32)
    for group_no in range(count):
        local_list.append(running_state)
        gain_list.append(running_gain)
        running_state = passing[group_no][:, None, None] * running_state + group_states[group_no]
        running_gain = passing[group_no] * running_gain
    blocks_n = lax.axis_size("seq")
    gain_row = jnp.broadcast_to(running_gain[:, None, None], (heads_here, 1, state_width))
    packed = jnp.concatenate([running_state, gain_row], 1)
    identity = jnp.concatenate([0.0 * running_state, 1.0 + 0.0 * gain_row], 1)
    late_piece, packed = lax.optimization_barrier((piece, packed))
    gate_turned = jnp.stack(
        [
            jnp.dot(
                w_gate.T,
                late_piece[group_no * GROUP : (group_no + 1) * GROUP].T,
                preferred_element_type=jnp.float32,
            )
            for group_no in range(rows_here // GROUP)
        ],
        0,
    )

    def joined_of(earlier_part, later_part):
        later_gain = later_part[:, head_width:, :]
        return jnp.concatenate(
            [
                later_gain * earlier_part[:, :head_width, :] + later_part[:, :head_width, :],
                later_gain * earlier_part[:, head_width:, :],
            ],
            1,
        )

    def fetched(part, by):
        return jnp.where(device >= by, shifted(part, "seq", by), identity)

    depth = min(blocks_n, LONG // rows_here)
    span = 1
    while span * span < depth:
        span += 1
    recent = identity
    for by in range(span, 0, -1):
        if by < blocks_n:
            recent = joined_of(recent, fetched(packed, by))
    prefix = recent
    for hop in range(1, (depth + span - 1) // span):
        if hop * span < blocks_n:
            prefix = joined_of(fetched(recent, hop * span), prefix)
    incoming = prefix[:, :head_width, :]
    entering = jnp.stack(gain_list, 0)[:, :, None, None] * incoming[None] + jnp.stack(local_list, 0)
    enter_weight = jnp.where((group_ids == prior_ids[:, None])[:, :, None], jnp.exp(cumul), 0.0)
    carried = (
        jnp.einsum("ctn,chpn->cthp", group_c, entering, precision=HIGH)
        * enter_weight[:, :, :, None]
    )
    end_state = (running_gain[:, None, None] * incoming + running_state)[None]
    heads_n = lax.axis_size("head")
    group_shape = (count, GROUP, heads_here, head_width)
    gate_act = jnp.transpose(
        jax.nn.silu(gate_turned).reshape(count, heads_here, head_width, GROUP), (0, 3, 1, 2)
    )
    direct = jnp.transpose(
        (skip_gain[:, None, None] * x_float).reshape(heads_here, head_width, count, GROUP), (2, 3, 0, 1)
    )
    gated = (within + carried + direct) * gate_act
    scaled = (gated * norm_gain.reshape(heads_here, head_width)).astype(jnp.bfloat16)
    partial_out = jnp.einsum(
        "cthp,hpo->cto",
        scaled,
        w_out.reshape(heads_here, head_width, w_out.shape[1]),
        preferred_element_type=jnp.float32,
    ).reshape(rows_here, w_out.shape[1])
    cols = partial_out.shape[1] // heads_n
    square_rows = jnp.sum(gated * gated, axis=(2, 3)).reshape(-1, cols)
    joined = jnp.concatenate([partial_out, jnp.tile(square_rows, (1, heads_n))], 0)
    summed = lax.psum_scatter(
        joined.astype(jnp.bfloat16), "head", scatter_dimension=1, tiled=True
    ).astype(jnp.float32)
    mean_square = (summed[rows_here:].reshape(rows_here) / INNER)[:, None]
    mixed = (summed[:rows_here] * lax.rsqrt(mean_square + EPSILON)).astype(jnp.bfloat16)
    return (mixed, end_state)


def solution(mesh):
    return jax.shard_map(
        shards,
        mesh=mesh,
        in_specs=(
            P("seq", "head"),
            P(),
            P(None, "head"),
            P(None, "head"),
            P(),
            P(None, "head"),
            P(None, "head"),
            P(),
            P("head"),
            P(),
            P("head"),
            P("head"),
            P("head"),
            P("head"),
            P("head", None),
        ),
        out_specs=(P("seq", "head"), P("seq", "head", None, None)),
        check_vma=False,
    )
```

```python
import jax
import jax.numpy as jnp
from jax import lax
from jax.sharding import PartitionSpec as P

GROUP = 256
INNER = 4096
LONG = 16384


EPSILON = 1e-05
HIGH = lax.Precision.HIGHEST


def shifted(x, axis, by):
    devices = lax.axis_size(axis)
    pairs = [(i, i + by) for i in range(devices) if 0 <= i + by < devices]
    return lax.ppermute(x, axis, pairs)


def carried_in(part, axis, combine, identity):
    place = lax.axis_index(axis)
    gathered = jax.tree.map(lambda a: lax.all_gather(a, axis), part)
    state = jax.tree.map(lambda a, e: jnp.zeros_like(a) + jnp.asarray(e, a.dtype), part, identity)

    def one(hop, state):
        return combine(
            state, jax.tree.map(lambda a: lax.dynamic_index_in_dim(a, hop, 0, False), gathered)
        )

    return lax.fori_loop(0, place, one, state)


def conv_block(projected, edge_rows, weights, offsets, idents, earlier):
    rows_here = projected.shape[0]
    lag_count = edge_rows.shape[0]
    joined = jnp.concatenate([edge_rows, projected], 0).astype(jnp.float32)
    joined_ids = jnp.concatenate([earlier, idents], 0)
    result = joined[lag_count:] * weights[0]
    for shift_by in range(1, lag_count + 1):
        window = joined[lag_count - shift_by : lag_count - shift_by + rows_here]
        matches = joined_ids[lag_count - shift_by : lag_count - shift_by + rows_here] == idents
        result = result + jnp.where(matches[:, None], window, 0.0) * weights[shift_by]
    return result + offsets


def conv_turned(projected, edge_rows, weights, offsets, idents, earlier):
    rows_here = projected.shape[1]
    lag_count = edge_rows.shape[0]
    joined = jnp.concatenate([edge_rows.T, projected], 1).astype(jnp.float32)
    joined_ids = jnp.concatenate([earlier, idents], 0)
    result = joined[:, lag_count:] * weights[0][:, None]
    for shift_by in range(1, lag_count + 1):
        window = joined[:, lag_count - shift_by : lag_count - shift_by + rows_here]
        matches = joined_ids[lag_count - shift_by : lag_count - shift_by + rows_here] == idents
        result = result + jnp.where(matches[None, :], window, 0.0) * weights[shift_by][:, None]
    return result + offsets[:, None]


def combine(earlier, later):
    return (earlier[0] * later[0], later[0][:, None, None] * earlier[1] + later[1])


def shards(
    tokens,
    seg_ids,
    w_gate,
    w_x,
    w_bc,
    w_dt,
    conv_x,
    conv_bc,
    conv_x_bias,
    conv_bc_bias,
    dt_bias,
    decay_rate,
    skip_gain,
    norm_gain,
    w_out,
):
    rows_here = tokens.shape[0]
    heads_here = w_dt.shape[1]
    inner_here = w_x.shape[1]
    head_width = inner_here // heads_here
    state_width = w_bc.shape[1] // 2
    lag_count = conv_x.shape[0] - 1
    device = lax.axis_index("seq")
    first_row = device * rows_here
    piece = lax.all_gather(tokens, "head", axis=1, tiled=True)

    def partial_product(matrix):
        return jnp.dot(piece, matrix, preferred_element_type=jnp.float32)

    x_turned = jnp.dot(w_x.T, piece.T, preferred_element_type=jnp.float32).astype(jnp.bfloat16)
    bc_sum = partial_product(w_bc)
    dt_raw = partial_product(w_dt)
    bc_pre = bc_sum.astype(jnp.bfloat16)
    idents = lax.dynamic_slice_in_dim(seg_ids, first_row, rows_here)
    earlier = lax.dynamic_slice_in_dim(seg_ids, jnp.maximum(first_row - lag_count, 0), lag_count)
    earlier = jnp.where(device > 0, earlier, -1)
    edges = shifted(
        jnp.concatenate([x_turned[:, rows_here - lag_count :].T, bc_pre[rows_here - lag_count :]], 1),
        "seq",
        1,
    )
    edge_x, edge_bc = edges[:, :inner_here], edges[:, inner_here:]
    x_conv = jax.nn.silu(
        conv_turned(x_turned, edge_x, conv_x, conv_x_bias, idents, earlier)
    ).astype(jnp.bfloat16)
    bc_conv = jax.nn.silu(
        conv_block(bc_pre, edge_bc, conv_bc, conv_bc_bias, idents, earlier)
    ).astype(jnp.bfloat16)
    steps_dt = jax.nn.softplus(dt_raw + dt_bias)
    log_decay = -steps_dt * decay_rate
    x_float = x_conv.astype(jnp.float32).reshape(heads_here, head_width, rows_here)
    x_scaled = x_float * steps_dt.T[:, None, :]
    count = rows_here // GROUP
    group_x = jnp.transpose(x_scaled.reshape(heads_here, head_width, count, GROUP), (2, 3, 0, 1))
    group_b = bc_conv[:, :state_width].astype(jnp.float32).reshape(count, GROUP, state_width)
    group_c = bc_conv[:, state_width:].astype(jnp.float32).reshape(count, GROUP, state_width)
    group_ids = idents.reshape(count, GROUP)
    cumul = jnp.cumsum(log_decay.reshape(count, GROUP, heads_here), axis=1)
    cumul_heads = jnp.transpose(cumul, (0, 2, 1))
    places = jnp.arange(GROUP)
    causal = places[None, :] <= places[:, None]
    linked = causal[None] & (group_ids[:, :, None] == group_ids[:, None, :])
    gaps = cumul_heads[:, :, :, None] - cumul_heads[:, :, None, :]
    link_heads = linked[:, None, :, :]
    decays = jnp.where(link_heads, jnp.exp(jnp.where(link_heads, gaps, 0.0)), 0.0)
    scores = jnp.einsum("ctn,csn->cts", group_c, group_b, precision=HIGH)
    within = jnp.einsum("chts,cshp->cthp", decays * scores[:, None, :, :], group_x, precision=HIGH)
    last_ids = group_ids[:, -1]
    tails = jnp.where(
        (group_ids == last_ids[:, None])[:, :, None], jnp.exp(cumul[:, -1:, :] - cumul), 0.0
    )
    group_states = jnp.einsum(
        "cshp,csn->chpn", group_x * tails[:, :, :, None], group_b, precision=HIGH
    )
    prior_ids = jnp.concatenate([earlier[-1:], last_ids[:-1]], 0)
    passing = jnp.where((last_ids == prior_ids)[:, None], jnp.exp(cumul[:, -1, :]), 0.0)
    local_list = []
    gain_list = []
    running_state = jnp.zeros((heads_here, head_width, state_width), jnp.float32)
    running_gain = jnp.ones((heads_here,), jnp.float32)
    for group_no in range(count):
        local_list.append(running_state)
        gain_list.append(running_gain)
        running_state = passing[group_no][:, None, None] * running_state + group_states[group_no]
        running_gain = passing[group_no] * running_gain
    blocks_n = lax.axis_size("seq")
    gain_row = jnp.broadcast_to(running_gain[:, None, None], (heads_here, 1, state_width))
    packed = jnp.concatenate([running_state, gain_row], 1)
    identity = jnp.concatenate([0.0 * running_state, 1.0 + 0.0 * gain_row], 1)
    late_piece, packed = lax.optimization_barrier((piece, packed))
    gate_turned = jnp.einsum(
        "ctd,dk->ckt",
        late_piece.reshape(rows_here // GROUP, GROUP, late_piece.shape[1]),
        w_gate,
        preferred_element_type=jnp.float32,
    )

    def joined_of(earlier_part, later_part):
        later_gain = later_part[:, head_width:, :]
        return jnp.concatenate(
            [
                later_gain * earlier_part[:, :head_width, :] + later_part[:, :head_width, :],
                later_gain * earlier_part[:, head_width:, :],
            ],
            1,
        )

    def fetched(part, by):
        return jnp.where(device >= by, shifted(part, "seq", by), identity)

    depth = min(blocks_n, LONG // rows_here)
    span = 1
    while span * span < depth:
        span += 1
    recent = identity
    for by in range(span, 0, -1):
        if by < blocks_n:
            recent = joined_of(recent, fetched(packed, by))
    prefix = recent
    for hop in range(1, (depth + span - 1) // span):
        if hop * span < blocks_n:
            prefix = joined_of(fetched(recent, hop * span), prefix)
    incoming = prefix[:, :head_width, :]
    entering = jnp.stack(gain_list, 0)[:, :, None, None] * incoming[None] + jnp.stack(local_list, 0)
    enter_weight = jnp.where((group_ids == prior_ids[:, None])[:, :, None], jnp.exp(cumul), 0.0)
    carried = (
        jnp.einsum("ctn,chpn->cthp", group_c, entering, precision=HIGH)
        * enter_weight[:, :, :, None]
    )
    end_state = (running_gain[:, None, None] * incoming + running_state)[None]
    heads_n = lax.axis_size("head")
    group_shape = (count, GROUP, heads_here, head_width)
    gate_act = jnp.transpose(
        jax.nn.silu(gate_turned).reshape(count, heads_here, head_width, GROUP), (0, 3, 1, 2)
    )
    direct = jnp.transpose(
        (skip_gain[:, None, None] * x_float).reshape(heads_here, head_width, count, GROUP), (2, 3, 0, 1)
    )
    gated = (within + carried + direct) * gate_act
    scaled = (gated * norm_gain.reshape(heads_here, head_width)).astype(jnp.bfloat16)
    partial_out = jnp.einsum(
        "cthp,hpo->cto",
        scaled,
        w_out.reshape(heads_here, head_width, w_out.shape[1]),
        preferred_element_type=jnp.float32,
    ).reshape(rows_here, w_out.shape[1])
    cols = partial_out.shape[1] // heads_n
    square_rows = jnp.sum(gated * gated, axis=(2, 3)).reshape(-1, cols)
    joined = jnp.concatenate([partial_out, jnp.tile(square_rows, (1, heads_n))], 0)
    summed = lax.psum_scatter(
        joined.astype(jnp.bfloat16), "head", scatter_dimension=1, tiled=True
    ).astype(jnp.float32)
    mean_square = (summed[rows_here:].reshape(rows_here) / INNER)[:, None]
    mixed = (summed[:rows_here] * lax.rsqrt(mean_square + EPSILON)).astype(jnp.bfloat16)
    return (mixed, end_state)


def solution(mesh):
    return jax.shard_map(
        shards,
        mesh=mesh,
        in_specs=(
            P("seq", "head"),
            P(),
            P(None, "head"),
            P(None, "head"),
            P(),
            P(None, "head"),
            P(None, "head"),
            P(),
            P("head"),
            P(),
            P("head"),
            P("head"),
            P("head"),
            P("head"),
            P("head", None),
        ),
        out_specs=(P("seq", "head"), P("seq", "head", None, None)),
        check_vma=False,
    )
```

```python
import jax
import jax.numpy as jnp
from jax import lax
from jax.sharding import PartitionSpec as P

GROUP = 256
INNER = 4096
LONG = 16384


EPSILON = 1e-05
HIGH = lax.Precision.HIGHEST


def shifted(x, axis, by):
    devices = lax.axis_size(axis)
    pairs = [(i, i + by) for i in range(devices) if 0 <= i + by < devices]
    return lax.ppermute(x, axis, pairs)


def carried_in(part, axis, combine, identity):
    place = lax.axis_index(axis)
    gathered = jax.tree.map(lambda a: lax.all_gather(a, axis), part)
    state = jax.tree.map(lambda a, e: jnp.zeros_like(a) + jnp.asarray(e, a.dtype), part, identity)

    def one(hop, state):
        return combine(
            state, jax.tree.map(lambda a: lax.dynamic_index_in_dim(a, hop, 0, False), gathered)
        )

    return lax.fori_loop(0, place, one, state)


def conv_block(projected, edge_rows, weights, offsets, idents, earlier):
    rows_here = projected.shape[0]
    lag_count = edge_rows.shape[0]
    joined = jnp.concatenate([edge_rows, projected], 0).astype(jnp.float32)
    joined_ids = jnp.concatenate([earlier, idents], 0)
    result = joined[lag_count:] * weights[0]
    for shift_by in range(1, lag_count + 1):
        window = joined[lag_count - shift_by : lag_count - shift_by + rows_here]
        matches = joined_ids[lag_count - shift_by : lag_count - shift_by + rows_here] == idents
        result = result + jnp.where(matches[:, None], window, 0.0) * weights[shift_by]
    return result + offsets


def combine(earlier, later):
    return (earlier[0] * later[0], later[0][:, None, None] * earlier[1] + later[1])


def shards(
    tokens,
    seg_ids,
    w_gate,
    w_x,
    w_bc,
    w_dt,
    conv_x,
    conv_bc,
    conv_x_bias,
    conv_bc_bias,
    dt_bias,
    decay_rate,
    skip_gain,
    norm_gain,
    w_out,
):
    rows_here = tokens.shape[0]
    heads_here = w_dt.shape[1]
    inner_here = w_x.shape[1]
    head_width = inner_here // heads_here
    state_width = w_bc.shape[1] // 2
    lag_count = conv_x.shape[0] - 1
    device = lax.axis_index("seq")
    first_row = device * rows_here
    piece = lax.all_gather(tokens, "head", axis=1, tiled=True)

    def partial_product(matrix):
        return jnp.dot(piece, matrix, preferred_element_type=jnp.float32)

    x_sum = partial_product(w_x)
    bc_sum = partial_product(w_bc)
    dt_raw = partial_product(w_dt)
    x_pre = x_sum.astype(jnp.bfloat16)
    bc_pre = bc_sum.astype(jnp.bfloat16)
    idents = lax.dynamic_slice_in_dim(seg_ids, first_row, rows_here)
    earlier = lax.dynamic_slice_in_dim(seg_ids, jnp.maximum(first_row - lag_count, 0), lag_count)
    earlier = jnp.where(device > 0, earlier, -1)
    edges = shifted(
        jnp.concatenate([x_pre[rows_here - lag_count :], bc_pre[rows_here - lag_count :]], 1),
        "seq",
        1,
    )
    edge_x, edge_bc = edges[:, :inner_here], edges[:, inner_here:]
    x_conv = jax.nn.silu(conv_block(x_pre, edge_x, conv_x, conv_x_bias, idents, earlier)).astype(
        jnp.bfloat16
    )
    bc_conv = jax.nn.silu(
        conv_block(bc_pre, edge_bc, conv_bc, conv_bc_bias, idents, earlier)
    ).astype(jnp.bfloat16)
    steps_dt = jax.nn.softplus(dt_raw + dt_bias)
    log_decay = -steps_dt * decay_rate
    x_float = x_conv.astype(jnp.float32).reshape(rows_here, heads_here, head_width)
    x_scaled = x_float * steps_dt[:, :, None]
    count = rows_here // GROUP
    group_x = x_scaled.reshape(count, GROUP, heads_here, head_width)
    group_b = bc_conv[:, :state_width].astype(jnp.float32).reshape(count, GROUP, state_width)
    group_c = bc_conv[:, state_width:].astype(jnp.float32).reshape(count, GROUP, state_width)
    group_ids = idents.reshape(count, GROUP)
    cumul = jnp.cumsum(log_decay.reshape(count, GROUP, heads_here), axis=1)
    cumul_heads = jnp.transpose(cumul, (0, 2, 1))
    places = jnp.arange(GROUP)
    causal = places[None, :] <= places[:, None]
    linked = causal[None] & (group_ids[:, :, None] == group_ids[:, None, :])
    gaps = cumul_heads[:, :, :, None] - cumul_heads[:, :, None, :]
    link_heads = linked[:, None, :, :]
    decays = jnp.where(link_heads, jnp.exp(jnp.where(link_heads, gaps, 0.0)), 0.0)
    scores = jnp.einsum("ctn,csn->cts", group_c, group_b, precision=HIGH)
    within = jnp.einsum("chts,cshp->cthp", decays * scores[:, None, :, :], group_x, precision=HIGH)
    last_ids = group_ids[:, -1]
    tails = jnp.where(
        (group_ids == last_ids[:, None])[:, :, None], jnp.exp(cumul[:, -1:, :] - cumul), 0.0
    )
    group_states = jnp.einsum(
        "cshp,csn->chpn", group_x * tails[:, :, :, None], group_b, precision=HIGH
    )
    prior_ids = jnp.concatenate([earlier[-1:], last_ids[:-1]], 0)
    passing = jnp.where((last_ids == prior_ids)[:, None], jnp.exp(cumul[:, -1, :]), 0.0)
    local_list = []
    gain_list = []
    running_state = jnp.zeros((heads_here, head_width, state_width), jnp.float32)
    running_gain = jnp.ones((heads_here,), jnp.float32)
    for group_no in range(count):
        local_list.append(running_state)
        gain_list.append(running_gain)
        running_state = passing[group_no][:, None, None] * running_state + group_states[group_no]
        running_gain = passing[group_no] * running_gain
    blocks_n = lax.axis_size("seq")
    gain_row = jnp.broadcast_to(running_gain[:, None, None], (heads_here, 1, state_width))
    packed = jnp.concatenate([running_state, gain_row], 1)
    identity = jnp.concatenate([0.0 * running_state, 1.0 + 0.0 * gain_row], 1)
    late_piece, packed = lax.optimization_barrier((piece, packed))
    gate_turned = jnp.stack(
        [
            jnp.dot(
                w_gate.T,
                late_piece[group_no * GROUP : (group_no + 1) * GROUP].T,
                preferred_element_type=jnp.float32,
            )
            for group_no in range(rows_here // GROUP)
        ],
        0,
    )

    def joined_of(earlier_part, later_part):
        later_gain = later_part[:, head_width:, :]
        return jnp.concatenate(
            [
                later_gain * earlier_part[:, :head_width, :] + later_part[:, :head_width, :],
                later_gain * earlier_part[:, head_width:, :],
            ],
            1,
        )

    def fetched(part, by):
        return jnp.where(device >= by, shifted(part, "seq", by), identity)

    depth = min(blocks_n, LONG // rows_here)
    span = 1
    while span * span < depth:
        span += 1
    recent = identity
    for by in range(span, 0, -1):
        if by < blocks_n:
            recent = joined_of(recent, fetched(packed, by))
    prefix = recent
    for hop in range(1, (depth + span - 1) // span):
        if hop * span < blocks_n:
            prefix = joined_of(fetched(recent, hop * span), prefix)
    incoming = prefix[:, :head_width, :]
    entering = jnp.stack(gain_list, 0)[:, :, None, None] * incoming[None] + jnp.stack(local_list, 0)
    enter_weight = jnp.where((group_ids == prior_ids[:, None])[:, :, None], jnp.exp(cumul), 0.0)
    carried = (
        jnp.einsum("ctn,chpn->cthp", group_c, entering, precision=HIGH)
        * enter_weight[:, :, :, None]
    )
    end_state = (running_gain[:, None, None] * incoming + running_state)[None]
    heads_n = lax.axis_size("head")
    group_shape = (count, GROUP, heads_here, head_width)
    gate_act = jnp.transpose(
        jax.nn.silu(gate_turned).reshape(count, heads_here, head_width, GROUP), (0, 3, 1, 2)
    )
    direct = skip_gain[:, None] * x_float.reshape(group_shape)
    gated = (within + carried + direct) * gate_act
    scaled = (gated * norm_gain.reshape(heads_here, head_width)).astype(jnp.bfloat16)
    partial_out = jnp.einsum(
        "cthp,hpo->cto",
        scaled,
        w_out.reshape(heads_here, head_width, w_out.shape[1]),
        preferred_element_type=jnp.float32,
    ).reshape(rows_here, w_out.shape[1])
    cols = partial_out.shape[1] // heads_n
    square_rows = jnp.sum(gated * gated, axis=(2, 3)).reshape(-1, cols)
    joined = jnp.concatenate([partial_out, jnp.tile(square_rows, (1, heads_n))], 0)
    summed = lax.psum_scatter(
        joined.astype(jnp.bfloat16), "head", scatter_dimension=1, tiled=True
    )
    mean_square = (summed[rows_here:].astype(jnp.float32).reshape(rows_here) / INNER)[:, None]
    mixed = (summed[:rows_here].astype(jnp.float32) * lax.rsqrt(mean_square + EPSILON)).astype(
        jnp.bfloat16
    )
    return (mixed, end_state)


def solution(mesh):
    return jax.shard_map(
        shards,
        mesh=mesh,
        in_specs=(
            P("seq", "head"),
            P(),
            P(None, "head"),
            P(None, "head"),
            P(),
            P(None, "head"),
            P(None, "head"),
            P(),
            P("head"),
            P(),
            P("head"),
            P("head"),
            P("head"),
            P("head"),
            P("head", None),
        ),
        out_specs=(P("seq", "head"), P("seq", "head", None, None)),
        check_vma=False,
    )
```
